32 devices in a mesh: seq: 8 (over z, x), head: 4 (over y, core).
Axes of the slice: x: 2, y: 2, z: 4, core: 2. Of those that a mesh axis runs over, the one named last changes fastest.
Arguments:
- queries: bfloat16 [6144, 2048], P('seq', 'head'), may hold values from -16 to 16
- key_rows: bfloat16 [6144, 2048], P('seq', 'head'), may hold values from -6 to 6
- value_rows: bfloat16 [6144, 2048], P('seq', 'head'), may hold values from -6 to 6
- out_weight: bfloat16 [2048, 3072], P('head'), may hold values from -0.125 to 0.125
- cotangent: bfloat16 [6144, 3072], P('seq', 'head'), may hold values from -6 to 6
- neighbours: int32 [16, 4], P('seq'), may hold values from -1 to 15, as said below
Outputs:
- projected: bfloat16 [6144, 3072], P('seq', 'head')
- grad_queries: bfloat16 [6144, 2048], P('seq', 'head')
- grad_keys: bfloat16 [6144, 2048], P('seq', 'head')
- grad_values: bfloat16 [6144, 2048], P('seq', 'head')
- grad_weight: float32 [2048, 3072], P('head', 'seq')
The draws below stay inside these ranges and needn't reach their ends.
Inputs may be any that keep to these rules, and one draw needn't show every extreme that they name: `neighbours`: slot 0 of tile t holds t; every other slot holds -1 or a tile other than t within 2 tiles of t, no tile twice in a row; the -1 slots of a row come after its tiles.
All inputs are finite; a program needn't handle non-finite values.
Results may differ from the reference program's by a relative error of at most 0.014.
Values may be sent and summed in bfloat16 or wider, within the bound.
A program may use at most 192 MiB of HBM per device.

```python
import math
import jax
import jax.numpy as jnp
from jax import lax

D = 3072
HEADS = 16
HD = 128
TILE = 384
REACH = 2
SLOTS = 4
TOKENS = 6144


def joint_draw(key):
    columns = HEADS * HD
    query_base = jnp.clip(jax.random.normal(jax.random.fold_in(key, 101), (TOKENS, columns), jnp.float32), -6.0, 6.0)
    key_base = jnp.clip(jax.random.normal(jax.random.fold_in(key, 102), (TOKENS, columns), jnp.float32), -6.0, 6.0)
    return (query_base, key_base)


def draw_queries(key, part):
    return joint_draw(key)[0].astype(jnp.bfloat16)


def draw_key_rows(key, part):
    return joint_draw(key)[1].astype(jnp.bfloat16)


def draw_neighbours(key, part):
    tile_total = TOKENS // TILE
    centre = jnp.arange(tile_total, dtype=jnp.int32)[:, None]
    near_offsets = jnp.array([-1, 1], jnp.int32)
    near_target = centre + near_offsets[None, :]
    near_inside = (near_target >= 0) & (near_target < tile_total)
    near = jnp.where(near_inside, near_target, -1)
    far_count = SLOTS - 3
    far_offsets = jnp.concatenate([jnp.arange(-REACH, -1, dtype=jnp.int32), jnp.arange(2, REACH + 1, dtype=jnp.int32)])
    far_total = far_offsets.shape[0]
    rank_keys = jax.random.randint(jax.random.fold_in(key, 201), (tile_total, far_total), 0, 4096) * max(far_total, 1) + jnp.arange(far_total, dtype=jnp.int32)[None, :]
    ordering = jnp.argsort(rank_keys, axis=1)
    far_target = jnp.take_along_axis(centre + far_offsets[None, :], ordering, 1)[:, :far_count]
    far_inside = (far_target >= 0) & (far_target < tile_total)
    kept = jax.random.randint(jax.random.fold_in(key, 202), (tile_total, far_count), 0, 4) != 0
    far = jnp.where(far_inside & kept, far_target, -1)
    others = jnp.concatenate([near, far], axis=1)
    width = SLOTS - 1
    sort_keys = jnp.where(others >= 0, 0, 1) * width + jnp.arange(width, dtype=jnp.int32)[None, :]
    compact = jnp.take_along_axis(others, jnp.argsort(sort_keys, axis=1), 1)
    return jnp.concatenate([centre, compact], axis=1).astype(jnp.int32)


def strengthened(values, own_key, source, target, parts, factor):
    owner, partner = [(jnp.arange(values.shape[axis_at]) // (values.shape[axis_at] // parts)).reshape([-1 if axis == axis_at else 1 for axis in range(values.ndim)]) for axis_at in (source, target)]
    chosen = jax.random.permutation(own_key, parts)[partner]
    strong = (owner == chosen) | (owner == (partner + parts // 2) % parts)
    return jnp.where(strong, factor * values, values)


def block_levels(stream_key, extent, split, least, high):
    factor_of = 1.0
    for position, parts in split:
        steps = jax.random.uniform(jax.random.fold_in(jax.random.fold_in(stream_key, 6), position), (parts,), jnp.float32, least / len(split), high / len(split))
        factor_of = factor_of * jnp.repeat(jnp.exp(steps), extent[position] // parts).reshape((-1,) + (1,) * (len(extent) - 1 - position))
    return factor_of


def centred(key, dims, scale, most, pieces=(), held_as=jnp.bfloat16):
    values = scale * jax.random.normal(key, dims, jnp.float32)
    if pieces:
        values = values * block_levels(key, dims, pieces, -0.22, 0.18)
    return jnp.clip(values, -most, most).astype(held_as)


def gaussian_with(own_key, dims, deviation, reach, shards, heavy, kind=jnp.bfloat16):
    values = deviation * jax.random.normal(own_key, dims, jnp.float32)
    if shards:
        values = values * block_levels(own_key, dims, shards, -0.22, 0.18)
    return jnp.clip(strengthened(values, jax.random.fold_in(own_key, 3), *heavy), -reach, reach).astype(kind)


def setup_inputs(seed: int = 0) -> dict:
    seeds = jax.random.split(jax.random.key(seed), 7)
    queries = draw_queries(jax.random.fold_in(seeds[6], 71), 0)
    key_rows = draw_key_rows(jax.random.fold_in(seeds[6], 71), 0)
    value_rows = centred(seeds[2], (TOKENS, HEADS * HD), 1.0, 6.0, ((0, 8), (1, 4)))
    out_weight = centred(seeds[3], (HEADS * HD, D), (HEADS * HD) ** -0.5, 0.125, ((0, 4),))
    cotangent = gaussian_with(seeds[4], (TOKENS, D), 1.0, 6.0, ((0, 8), (1, 4)), (0, 1, 8, 2.0))
    neighbours = draw_neighbours(jax.random.fold_in(seeds[6], 71), 0)
    return {"queries": queries, "key_rows": key_rows, "value_rows": value_rows, "out_weight": out_weight, "cotangent": cotangent, "neighbours": neighbours}


def reference(queries, key_rows, value_rows, out_weight, cotangent, neighbours):
    columns = HEADS * HD
    score_scale = 1.0 / math.sqrt(HD)
    tile_total = TOKENS // TILE
    grad_attention = jnp.dot(cotangent, out_weight.T, preferred_element_type=jnp.float32).astype(jnp.bfloat16)

    def per_tile(carry, tile_index):
        acc_keys, acc_values = carry
        start_row = (tile_index * TILE).astype(jnp.int32)
        query_tile = lax.dynamic_slice_in_dim(queries, start_row, TILE, 0).astype(jnp.float32).reshape(TILE, HEADS, HD)
        grad_tile = lax.dynamic_slice_in_dim(grad_attention, start_row, TILE, 0).astype(jnp.float32).reshape(TILE, HEADS, HD)
        key_list = []
        value_list = []
        live_list = []
        for slot_index in range(SLOTS):
            neighbour = neighbours[tile_index, slot_index]
            safe_start = (jnp.maximum(neighbour, 0) * TILE).astype(jnp.int32)
            key_list.append(lax.dynamic_slice_in_dim(key_rows, safe_start, TILE, 0))
            value_list.append(lax.dynamic_slice_in_dim(value_rows, safe_start, TILE, 0))
            live_list.append(jnp.broadcast_to(neighbour >= 0, (TILE,)))
        key_block = jnp.concatenate(key_list, 0).astype(jnp.float32).reshape(SLOTS * TILE, HEADS, HD)
        value_block = jnp.concatenate(value_list, 0).astype(jnp.float32).reshape(SLOTS * TILE, HEADS, HD)
        live_keys = jnp.concatenate(live_list, 0)
        scores = jnp.einsum('rhd,khd->hrk', query_tile, key_block) * score_scale
        scores = jnp.where(live_keys[None, None, :], scores, -1e+30)
        row_peak = lax.optimization_barrier(jnp.max(scores, axis=-1, keepdims=True))
        log_total = row_peak + jnp.log(lax.optimization_barrier(jnp.sum(jnp.exp(scores - row_peak), axis=-1, keepdims=True)))
        probabilities = jnp.exp(scores - log_total)
        probs_low = lax.optimization_barrier(probabilities.astype(jnp.bfloat16)).astype(jnp.float32)
        attention_tile = jnp.einsum('hrk,khd->rhd', probs_low, value_block).astype(jnp.bfloat16)
        attention_wide = lax.optimization_barrier(attention_tile).astype(jnp.float32)
        row_delta = lax.optimization_barrier(jnp.sum(grad_tile * attention_wide, axis=-1))
        grad_probs = jnp.einsum('rhd,khd->hrk', grad_tile, value_block)
        grad_scores = probabilities * (grad_probs - jnp.transpose(row_delta)[:, :, None])
        grad_scores = lax.optimization_barrier(grad_scores.astype(jnp.bfloat16)).astype(jnp.float32)
        grad_query = (jnp.einsum('hrk,khd->rhd', grad_scores, key_block) * score_scale).astype(jnp.bfloat16)
        grad_key_block = jnp.einsum('hrk,rhd->khd', grad_scores, query_tile) * score_scale
        grad_value_block = jnp.einsum('hrk,rhd->khd', probs_low, grad_tile)
        for slot_index in range(SLOTS):
            neighbour = neighbours[tile_index, slot_index]
            live_factor = (neighbour >= 0).astype(jnp.float32)
            safe_start = (jnp.maximum(neighbour, 0) * TILE).astype(jnp.int32)
            piece_keys = grad_key_block[slot_index * TILE:(slot_index + 1) * TILE].reshape(TILE, columns) * live_factor
            piece_values = grad_value_block[slot_index * TILE:(slot_index + 1) * TILE].reshape(TILE, columns) * live_factor
            acc_keys = lax.dynamic_update_slice_in_dim(acc_keys, lax.dynamic_slice_in_dim(acc_keys, safe_start, TILE, 0) + piece_keys, safe_start, 0)
            acc_values = lax.dynamic_update_slice_in_dim(acc_values, lax.dynamic_slice_in_dim(acc_values, safe_start, TILE, 0) + piece_values, safe_start, 0)
        return ((acc_keys, acc_values), (attention_tile.reshape(TILE, columns), grad_query.reshape(TILE, columns)))
    empty_acc = jnp.zeros((TOKENS, columns), jnp.float32)
    carried, stacked = lax.scan(per_tile, (empty_acc, empty_acc), jnp.arange(tile_total, dtype=jnp.int32))
    acc_keys, acc_values = carried
    attention_tiles, grad_query_tiles = stacked
    attention = attention_tiles.reshape(TOKENS, columns)
    projected = jnp.dot(attention, out_weight, preferred_element_type=jnp.float32).astype(jnp.bfloat16)
    grad_weight = jnp.dot(attention.T, cotangent, preferred_element_type=jnp.float32) * (1.0 / math.sqrt(TOKENS))
    return (projected, grad_query_tiles.reshape(TOKENS, columns), acc_keys.astype(jnp.bfloat16), acc_values.astype(jnp.bfloat16), grad_weight)
```

```python
import functools
import math

import jax
import jax.numpy as jnp
from jax import lax
from jax.experimental import pallas as pl
from jax.experimental.pallas import tpu as pltpu
from jax.sharding import PartitionSpec as P

HD = 128
TILE = 384
REACH = 2
SLOTS = 4
RIM = REACH * TILE
F32 = jnp.float32
BF16 = jnp.bfloat16


def dot_nt(a, b):
    return lax.dot_general(a, b, (((1,), (1,)), ((), ())), preferred_element_type=F32)


def dot_nn(a, b):
    return lax.dot_general(a, b, (((1,), (0,)), ((), ())), preferred_element_type=F32)


def dot_tn(a, b):
    return lax.dot_general(a, b, (((0,), (0,)), ((), ())), preferred_element_type=F32)


def fold(op, x):
    out = x[:, :HD]
    for i in range(1, x.shape[1] // HD):
        out = op(out, x[:, i * HD : (i + 1) * HD])
    return out


def attend(rows, tiles, place, count, q, g, km, vm, far, near, att, dq, mid, rim_far, rim_near, kx, vx, dk, dv, scr):
    t = pl.program_id(1)
    scale = 1.0 / math.sqrt(HD)
    c = scale * math.log2(math.e)
    hi = RIM + rows

    @pl.when(t == 0)
    def _():
        kx[:RIM] = far[0]
        kx[RIM:hi] = km[...]
        kx[hi:] = near[0]
        vx[:RIM] = far[1]
        vx[RIM:hi] = vm[...]
        vx[hi:] = near[1]
        dk[...] = jnp.zeros_like(dk)
        dv[...] = jnp.zeros_like(dv)

    live = count[t]
    qv = q[...]
    gv = g[...]

    def at(j):
        return pl.ds(pl.multiple_of(place[t * SLOTS + j] * TILE, TILE), TILE)

    def slots(step, carry):
        for j in range(SLOTS):
            carry = step(j, carry)
        return carry

    def score(j, m):
        s = dot_nt(qv, kx[at(j), :])
        if j:
            s = jnp.where(j < live, s, -1e30)
        scr[j] = s
        return jnp.maximum(m, fold(jnp.maximum, s))

    m = slots(score, jnp.full((TILE, HD), -3e38, F32))
    m = jnp.max(m, axis=1, keepdims=True)

    def soft(j, carry):
        total, acc = carry
        e = jnp.exp2((scr[j] - m) * c)
        scr[j] = e
        return total + fold(jnp.add, e), acc + dot_nn(e.astype(BF16), vx[at(j), :])

    zero = jnp.zeros((TILE, HD), F32)
    total, acc = slots(soft, (zero, zero))
    inv = 1.0 / jnp.sum(total, axis=1, keepdims=True)
    out = (acc * inv).astype(BF16)
    att[...] = out
    delta = jnp.sum(gv.astype(F32) * out.astype(F32), axis=1, keepdims=True)

    def back(j, acc):
        here = at(j)
        k = kx[here, :]
        p = scr[j] * inv
        ds = (p * (dot_nt(gv, vx[here, :]) - delta)).astype(BF16)
        dv[here, :] += dot_tn(p.astype(BF16), gv)
        dk[here, :] += dot_tn(ds, qv)
        return acc + dot_nn(ds, k)

    dq[...] = (slots(back, zero) * scale).astype(BF16)

    @pl.when(t == tiles - 1)
    def _():
        rim_far[0] = (dk[:RIM] * scale).astype(BF16)
        rim_far[1] = dv[:RIM].astype(BF16)
        mid[0] = dk[RIM:hi] * scale
        mid[1] = dv[RIM:hi]
        rim_near[0] = dk[hi:] * scale
        rim_near[1] = dv[hi:]


def attention_call(place, count, q, g, k, v, far, near, first, heads):
    rows = q.shape[0]
    tiles = rows // TILE
    ext = rows + 2 * RIM
    cols = heads * HD
    tile_in = pl.BlockSpec((TILE, HD), lambda h, t, *_: (t, first + h))
    slab_in = pl.BlockSpec((rows, HD), lambda h, t, *_: (0, first + h))
    rim = pl.BlockSpec((2, RIM, HD), lambda h, t, *_: (0, 0, h))
    tile_out = pl.BlockSpec((TILE, HD), lambda h, t, *_: (t, h))
    mid = pl.BlockSpec((2, rows, HD), lambda h, t, *_: (0, 0, h))
    pairs = heads * tiles * SLOTS
    return pl.pallas_call(
        functools.partial(attend, rows, tiles),
        grid_spec=pltpu.PrefetchScalarGridSpec(
            num_scalar_prefetch=2,
            grid=(heads, tiles),
            in_specs=[tile_in, tile_in, slab_in, slab_in, rim, rim],
            out_specs=[tile_out, tile_out, mid, rim, rim],
            scratch_shapes=[
                pltpu.VMEM((ext, HD), BF16),
                pltpu.VMEM((ext, HD), BF16),
                pltpu.VMEM((ext, HD), F32),
                pltpu.VMEM((ext, HD), F32),
                pltpu.VMEM((SLOTS, TILE, TILE), F32),
            ],
        ),
        out_shape=[
            jax.ShapeDtypeStruct((rows, cols), BF16),
            jax.ShapeDtypeStruct((rows, cols), BF16),
            jax.ShapeDtypeStruct((2, rows, cols), F32),
            jax.ShapeDtypeStruct((2, RIM, cols), BF16),
            jax.ShapeDtypeStruct((2, RIM, cols), F32),
        ],
        compiler_params=pltpu.CompilerParams(
            dimension_semantics=("arbitrary", "arbitrary"), vmem_limit_bytes=40 << 20
        ),
        cost_estimate=pl.CostEstimate(
            flops=pairs * 12 * TILE * TILE * HD,
            bytes_accessed=rows * cols * 40,
            transcendentals=pairs * TILE * TILE,
        ),
    )(place, count, q, g, k, v, far, near)


def swap(x, axis, bit):
    return lax.ppermute(x, axis, [(i, i ^ bit) for i in range(lax.axis_size(axis))])


def shift(x, axis, even_step):
    size = lax.axis_size(axis)
    pairs = [(i, i + (even_step if i % 2 == 0 else -even_step)) for i in range(size)]
    return lax.ppermute(x, axis, [(i, j) for i, j in pairs if 0 <= j < size])


MESH = pl.DeviceIdType.MESH

def mega(
    q_hbm, k_hbm, v_hbm, w_hbm, c_hbm, nb,
    proj_hbm, dq_hbm, dk_hbm, dv_hbm, gw_hbm,
    q, kx, vx, cot, w, g, att, dq, e, scr, st, ak, av,
    far_out, far_in, near_out, near_in, wx_out, wx_in, two_out, two_in, keep, four_out, four_in, gw,
    core_out, core_in, y_out, y_in,
    loc_s, out_s, kv_s, kv_r, fw_s, fw_r, cy_s, cy_r, cc_s, cc_r, rf_s, rf_r, rn_s, rn_r,
    wx_s, wx_r, two_s, two_r, four_s, four_r, co_s, co_r, y_s, y_r,
    *, seq, norm,
):
    s, h = lax.axis_index("seq"), lax.axis_index("head")
    x, z0, z1 = s % 2, (s // 2) % 2, (s // 4) % 2
    h0, h1 = h % 2, (h // 2) % 2
    beside = (s + 1 - 2 * x, h)
    hop2 = (s + 2 - 4 * z0, h)
    hop4 = (s + 4 - 8 * z1, h)
    mate = (s, h + 1 - 2 * h0)
    across = (s, h + 2 - 4 * h1)
    rows, cols = q.shape
    heads = cols // HD
    tiles = rows // TILE
    width = proj_hbm.shape[1]
    piece = gw_hbm.shape[1]
    scale = 1.0 / math.sqrt(HD)
    c2 = scale * math.log2(math.e)
    up, down = s + 2 - 4 * x, s - 2 + 4 * x
    has_up = (up >= 0) & (up < seq)
    has_down = (down >= 0) & (down < seq)

    def slab(i):
        return pl.ds(pl.multiple_of(i * rows, TILE), rows)

    far_at, near_at, mid_at = slab(2 * x), slab(2 - 2 * x), pl.ds(rows, rows)

    def send(src, dst, sem_s, sem_r, dev):
        return pltpu.make_async_remote_copy(
            src_ref=src, dst_ref=dst, send_sem=sem_s, recv_sem=sem_r,
            device_id=dev, device_id_type=MESH,
        )

    def hcol(i):
        return slice(i * HD, (i + 1) * HD)

    local = [pltpu.make_async_copy(c_hbm, cot.at[0], loc_s.at[0]),
             pltpu.make_async_copy(q_hbm, q, loc_s.at[1]),
             pltpu.make_async_copy(w_hbm, w, loc_s.at[2])]
    for i in range(heads):
        local.append(pltpu.make_async_copy(k_hbm.at[:, hcol(i)], kx.at[i, mid_at], loc_s.at[3 + 2 * i]))
        local.append(pltpu.make_async_copy(v_hbm.at[:, hcol(i)], vx.at[i, mid_at], loc_s.at[4 + 2 * i]))
    for copy in local:
        copy.start()

    @pl.when(jnp.logical_not(has_down))
    def _():
        for i in range(heads):
            kx[i, far_at] = jnp.zeros((rows, HD), BF16)
            vx[i, far_at] = jnp.zeros((rows, HD), BF16)

    barrier = pltpu.get_barrier_semaphore()
    for dev in (beside, hop4, mate, across):
        pl.semaphore_signal(barrier, inc=1, device_id=dev, device_id_type=MESH)

    @pl.when(s >= 2)
    def _():
        pl.semaphore_signal(barrier, inc=1, device_id=(s - 2, h), device_id_type=MESH)

    @pl.when(s + 2 < seq)
    def _():
        pl.semaphore_signal(barrier, inc=1, device_id=(s + 2, h), device_id_type=MESH)

    pl.semaphore_wait(barrier, 4 + (s + seq - 2) // seq + (2 * seq - 3 - s) // seq)

    kv, fw = [], []
    for i in range(heads):
        for n, (src, buf) in enumerate(((k_hbm, kx), (v_hbm, vx))):
            kv.append(send(src.at[:, hcol(i)], buf.at[i, slab(2 * x)], kv_s.at[2 * i + n], kv_r.at[2 * i + n], beside))
            fw.append(send(buf.at[i, near_at], buf.at[i, far_at], fw_s.at[2 * i + n], fw_r.at[2 * i + n], (up, h)))
    tile_rows = [pl.ds(t * TILE, TILE) for t in range(tiles)]
    cy = [send(c_hbm.at[r], cot.at[2, r], cy_s.at[t], cy_r.at[t], across) for t, r in enumerate(tile_rows)]
    cc = [send(cot.at[2, r], cot.at[3, r], cc_s.at[t], cc_r.at[t], mate) for t, r in enumerate(tile_rows)]
    cm = send(c_hbm, cot.at[1], cc_s.at[tiles], cc_r.at[tiles], mate)
    for copy in kv[:2] + cy + [cm] + kv[2:]:
        copy.start()

    def forward_halo(i):
        for n in range(2):
            kv[2 * i + n].wait_recv()

            @pl.when(has_up)
            def _():
                fw[2 * i + n].start()

    def halo(i):
        @pl.when(has_down)
        def _():
            for n in range(2):
                fw[2 * i + n].wait_recv()

    def dead(t, c):
        cand = s * tiles - REACH + t + c
        hit = sum(((nb[t, j] == cand) & (cand >= 0)).astype(jnp.int32) for j in range(SLOTS))
        return (1 - hit).astype(F32) * 1e30

    def cand(t, c):
        return pl.ds((t + c) * TILE, TILE)

    spread = 2 * REACH + 1

    def fwd(i):
        for t in range(tiles):
            at = tile_rows[t]
            qv = q[at, hcol(i)]
            m = jnp.full((8, TILE), -3e38, F32)
            off = [dead(t, c) for c in range(spread)]
            for c in range(spread):
                sc = dot_nt(kx[i, cand(t, c), :], qv)
                scr[t % 2, c] = sc
                m = jnp.maximum(m, jnp.max(sc.reshape(TILE // 8, 8, TILE), axis=0) - off[c])
            m = jnp.max(m, axis=0, keepdims=True) * c2
            total = jnp.zeros((8, TILE), F32)
            acc = jnp.zeros((TILE, HD), F32)
            for c in range(spread):
                p = jnp.exp2(scr[t % 2, c] * c2 - (m + off[c]))
                total = total + jnp.sum(p.reshape(TILE // 8, 8, TILE), axis=0)
                low = p.astype(BF16)
                e[i % 2, t, c] = low
                acc = acc + dot_tn(low, vx[i, cand(t, c), :])
            inv = jnp.broadcast_to(1.0 / jnp.sum(total, axis=0, keepdims=True), (HD, TILE)).T
            att[at, hcol(i)] = (acc * inv).astype(BF16)
            st[i % 2, t] = inv

    def bwd(i):
        for t in range(tiles):
            at = tile_rows[t]
            qv = q[at, hcol(i)]
            gv = g[at, hcol(i)].astype(F32) * st[i % 2, t]
            delta = jnp.sum((gv * att[at, hcol(i)].astype(F32)).T, axis=0, keepdims=True)
            gb = gv.astype(BF16)
            acc = jnp.zeros((TILE, HD), F32)
            for c in range(spread):
                here = cand(t, c)
                p = e[i % 2, t, c]
                ds = (p.astype(F32) * (dot_nt(vx[i, here, :], gb) - delta)).astype(BF16)
                if t == 0 or c == spread - 1:
                    av[i, here, :] = dot_nn(p, gb)
                    ak[i, here, :] = dot_nn(ds, qv)
                else:
                    av[i, here, :] += dot_nn(p, gb)
                    ak[i, here, :] += dot_nn(ds, qv)
                acc = acc + dot_tn(ds, kx[i, here, :])
            dq[at, hcol(i)] = (acc * scale).astype(BF16)

    rf = [send(far_out.at[i], far_in.at[i], rf_s.at[i], rf_r.at[i], (down, h)) for i in range(heads)]
    rn = [send(near_out.at[i], near_in.at[i], rn_s.at[i], rn_r.at[i], beside) for i in range(heads)]

    def send_far(i):
        @pl.when(has_down)
        def _():
            far_out[i, 0] = (ak[i, far_at] * scale).astype(BF16)
            far_out[i, 1] = av[i, far_at].astype(BF16)
            rf[i].start()

    def relay(i):
        @pl.when(has_up)
        def _():
            rf[i].wait_recv()
            near_out[i, 0] = (ak[i, near_at] * scale + far_in[i, 0].astype(F32)).astype(BF16)
            near_out[i, 1] = (av[i, near_at] + far_in[i, 1].astype(F32)).astype(BF16)

        @pl.when(jnp.logical_not(has_up))
        def _():
            near_out[i, 0] = (ak[i, near_at] * scale).astype(BF16)
            near_out[i, 1] = av[i, near_at].astype(BF16)

        rn[i].start()

    outs = []

    def write(src, dst):
        copy = pltpu.make_async_copy(src, dst, out_s.at[len(outs)])
        copy.start()
        outs.append(copy)

    def settle(i):
        @pl.when(has_down)
        def _():
            rf[i].wait_send()

        rn[i].wait_recv()
        far_out[i, 0] = (ak[i, mid_at] * scale + near_in[i, 0].astype(F32)).astype(BF16)
        far_out[i, 1] = (av[i, mid_at] + near_in[i, 1].astype(F32)).astype(BF16)
        write(far_out.at[i, 0], dk_hbm.at[:, hcol(i)])
        write(far_out.at[i, 1], dv_hbm.at[:, hcol(i)])

    per = 2
    pairs = heads // per

    def term(p, k, side):
        r = (h0 + z0 + k % 2) % 2 + 2 * ((h1 + z1 + k // 2) % 2)
        a = att[:, p * per * HD : (p + 1) * per * HD]
        return dot_tn(a, cot[r, :, pl.ds(pl.multiple_of(side * piece, piece), piece)])

    wx = [send(wx_out.at[p], wx_in.at[p], wx_s.at[p], wx_r.at[p], beside) for p in range(pairs)]
    twos = [send(two_out.at[p], two_in.at[p], two_s.at[p], two_r.at[p], hop2) for p in range(pairs)]
    fours = [send(four_out.at[p], four_in.at[p], four_s.at[p], four_r.at[p], hop4) for p in range(pairs)]

    def weight_x(p):
        for k in range(4):
            wx_out[p, k] = term(p, k, 1 - x).astype(BF16)
        wx[p].start()

    def weight_two(p):
        own = [term(p, k, x) for k in range(4)]
        wx[p].wait_recv()
        for n, k in enumerate((1, 3)):
            two_out[p, n] = (own[k] + wx_in[p, k].astype(F32)).astype(BF16)
        twos[p].start()
        for n, k in enumerate((0, 2)):
            keep[p, n] = own[k] + wx_in[p, k].astype(F32)

    def weight_four(p):
        twos[p].wait_recv()
        four_out[p] = (keep[p, 1] + two_in[p, 1].astype(F32)).astype(BF16)
        fours[p].start()
        keep[p, 0] += two_in[p, 0].astype(F32)

    def weight_done(p):
        fours[p].wait_recv()
        at = slice(p * per * HD, (p + 1) * per * HD)
        gw[at] = (keep[p, 0] + four_in[p].astype(F32)) * norm
        write(gw.at[at], gw_hbm.at[at])

    def wcols(r):
        b0, b1 = (h0 + r % 2) % 2, (h1 + r // 2) % 2
        return pl.ds(pl.multiple_of((b0 + 2 * b1) * width, width), width)

    def share(t, r):
        return dot_nn(att[tile_rows[t], :], w[:, wcols(r)])

    cores = [[send(core_out.at[n, t], core_in.at[n, t], co_s.at[n, t], co_r.at[n, t], mate) for t in range(tiles)]
             for n in range(2)]
    ys = [send(y_out.at[t], y_in.at[t], y_s.at[t], y_r.at[t], across) for t in range(tiles)]

    def project_out():
        for n, r in enumerate((3, 1)):
            for t in range(tiles):
                core_out[n, t] = share(t, r).astype(BF16)
                cores[n][t].start()
        for t in range(tiles):
            total = share(t, 2)
            cores[0][t].wait_recv()
            y_out[t] = (total + core_in[0, t].astype(F32)).astype(BF16)
            ys[t].start()

    def project_in(t):
        total = share(t, 0)
        cores[1][t].wait_recv()
        ys[t].wait()
        y_out[t] = (total + core_in[1, t].astype(F32) + y_in[t].astype(F32)).astype(BF16)
        write(y_out.at[t], proj_hbm.at[tile_rows[t]])

    def grad_attention(t):
        total = dot_nt(cot[0, tile_rows[t]], w[:, wcols(0)])
        for r in range(1, 4):
            total += dot_nt(cot[r, tile_rows[t]], w[:, wcols(r)])
        g[tile_rows[t], :] = total.astype(BF16)

    forward_halo(0)
    for copy in local:
        copy.wait()
    cy[0].wait_recv()
    cc[0].start()
    forward_halo(1)
    halo(0)
    fwd(0)
    forward_halo(2)
    cy[1].wait_recv()
    cc[1].start()
    halo(1)
    fwd(1)
    cm.wait_recv()
    cc[0].wait_recv()
    cc[1].wait_recv()
    weight_x(0)
    for t in range(tiles):
        grad_attention(t)
    forward_halo(3)
    bwd(0)
    send_far(0)
    halo(2)
    fwd(2)
    bwd(1)
    send_far(1)
    relay(0)
    halo(3)
    fwd(3)
    bwd(2)
    send_far(2)
    relay(1)
    weight_x(1)
    bwd(3)
    send_far(3)
    write(dq, dq_hbm)
    weight_two(0)
    project_out()
    relay(2)
    relay(3)
    weight_four(0)
    settle(0)
    settle(1)
    weight_two(1)
    weight_done(0)
    for t in range(tiles):
        project_in(t)
    weight_four(1)
    settle(2)
    weight_done(1)
    settle(3)

    for copy in outs:
        copy.wait()

    @pl.when(has_up)
    def _():
        for copy in fw:
            copy.wait_send()

    for copy in kv + cy + cc + [cm] + rn + wx + twos + fours + cores[0] + cores[1]:
        copy.wait_send()


def mega_call(q, k, v, w, c, nb, seq, norm):
    rows, cols = q.shape
    heads = cols // HD
    tiles = rows // TILE
    width = c.shape[1]
    piece = width * 4 // seq
    pairs = heads // 2
    ext = 3 * rows
    spread = 2 * REACH + 1
    hbm = pl.BlockSpec(memory_space=pl.ANY)
    sem = pltpu.SemaphoreType.DMA
    vm = pltpu.VMEM
    return pl.pallas_call(
        functools.partial(mega, seq=seq, norm=norm),
        in_specs=[hbm] * 5 + [pl.BlockSpec(memory_space=pltpu.SMEM)],
        out_specs=[hbm] * 5,
        out_shape=[
            jax.ShapeDtypeStruct((rows, width), BF16),
            jax.ShapeDtypeStruct((rows, cols), BF16),
            jax.ShapeDtypeStruct((rows, cols), BF16),
            jax.ShapeDtypeStruct((rows, cols), BF16),
            jax.ShapeDtypeStruct((cols, piece), F32),
        ],
        scratch_shapes=[
            vm((rows, cols), BF16),
            vm((heads, ext, HD), BF16),
            vm((heads, ext, HD), BF16),
            vm((4, rows, width), BF16),
            vm(w.shape, BF16),
            vm((rows, cols), BF16),
            vm((rows, cols), BF16),
            vm((rows, cols), BF16),
            vm((2, tiles, spread, TILE, TILE), BF16),
            vm((2, spread, TILE, TILE), F32),
            vm((2, tiles, TILE, HD), F32),
            vm((heads, ext, HD), F32),
            vm((heads, ext, HD), F32),
            vm((heads, 2, rows, HD), BF16),
            vm((heads, 2, rows, HD), BF16),
            vm((heads, 2, rows, HD), BF16),
            vm((heads, 2, rows, HD), BF16),
            vm((pairs, 4, 2 * HD, piece), BF16),
            vm((pairs, 4, 2 * HD, piece), BF16),
            vm((pairs, 2, 2 * HD, piece), BF16),
            vm((pairs, 2, 2 * HD, piece), BF16),
            vm((pairs, 2, 2 * HD, piece), F32),
            vm((pairs, 2 * HD, piece), BF16),
            vm((pairs, 2 * HD, piece), BF16),
            vm((cols, piece), F32),
            vm((2, tiles, TILE, width), BF16),
            vm((2, tiles, TILE, width), BF16),
            vm((tiles, TILE, width), BF16),
            vm((tiles, TILE, width), BF16),
            sem((3 + 2 * heads,)), sem((1 + 2 * heads + pairs + tiles,)),
            sem((2 * heads,)), sem((2 * heads,)), sem((2 * heads,)), sem((2 * heads,)),
            sem((tiles,)), sem((tiles,)), sem((tiles + 1,)), sem((tiles + 1,)),
            sem((heads,)), sem((heads,)), sem((heads,)), sem((heads,)),
            sem((pairs,)), sem((pairs,)), sem((pairs,)), sem((pairs,)), sem((pairs,)), sem((pairs,)),
            sem((2, tiles)), sem((2, tiles)), sem((tiles,)), sem((tiles,)),
        ],
        compiler_params=pltpu.CompilerParams(
            collective_id=0, has_side_effects=True, vmem_limit_bytes=62 << 20
        ),
        cost_estimate=pl.CostEstimate(
            flops=16 * rows * cols * width * 3, bytes_accessed=40 << 20, transcendentals=0
        ),
    )(q, k, v, w, c, nb)


def local(queries, key_rows, value_rows, out_weight, cotangent, neighbours):
    rows, columns = queries.shape
    heads = columns // HD
    tiles = rows // TILE
    seq, head = lax.axis_size("seq"), lax.axis_size("head")
    s = lax.axis_index("seq")
    norm = 1.0 / math.sqrt(rows * seq)
    chunks = 2
    per = heads // chunks
    if head == 4 and seq == 8 and heads == 4 and tiles == REACH:
        return tuple(
            mega_call(queries, key_rows, value_rows, out_weight, cotangent, neighbours, seq, norm)
        )

    halos = []
    for n in range(chunks):
        cut = slice(n * per * HD, (n + 1) * per * HD)
        kv = jnp.stack([key_rows[:, cut], value_rows[:, cut]])
        near = swap(kv, "seq", 1)
        far = shift(near, "seq", 2)
        halos.append((far, near))

    full = lax.all_gather(cotangent, "head", axis=1, tiled=True)
    grad_attention = dot_nt(full, out_weight).astype(BF16)

    first = s * tiles - REACH
    alive = neighbours >= 0
    index = jnp.where(alive, neighbours - first, 0)
    span = tiles + REACH
    odd = s % 2 == 1
    turned = jnp.where(index < REACH, index + span, jnp.where(index >= span, index - span, index))
    place = jnp.where(odd, turned, index).reshape(-1).astype(jnp.int32)
    count = jnp.sum(alive, axis=1).astype(jnp.int32)

    atts, dqs, mids, fars, nears = [], [], [], [], []
    for n in range(chunks):
        far, near = halos[n]
        att, dq, mid, rim_far, rim_near = attention_call(
            place, count, queries, grad_attention, key_rows, value_rows, far, near, n * per, per
        )
        atts.append(att)
        dqs.append(dq)
        mids.append(mid)
        fars.append(rim_far)
        nears.append(rim_near)

    grad_queries = jnp.concatenate(dqs, axis=1)
    dks, dvs = [], []
    for n in range(chunks):
        relayed = shift(fars[n], "seq", -2)
        back = swap((nears[n] + relayed.astype(F32)).astype(BF16), "seq", 1)
        done = (mids[n] + back.astype(F32)).astype(BF16)
        dks.append(done[0])
        dvs.append(done[1])
    attention = jnp.concatenate(atts, axis=1)
    projected = lax.psum_scatter(
        dot_nn(attention, out_weight).astype(BF16), "head", scatter_dimension=1, tiled=True
    )
    grad_weight = (
        lax.psum_scatter(
            dot_tn(attention, full).astype(BF16), "seq", scatter_dimension=1, tiled=True
        ).astype(F32)
        * norm
    )
    return (
        projected,
        grad_queries,
        jnp.concatenate(dks, axis=1),
        jnp.concatenate(dvs, axis=1),
        grad_weight,
    )


def solution(mesh):
    both = P("seq", "head")
    return jax.shard_map(
        local,
        mesh=mesh,
        in_specs=(both, both, both, P("head", None), both, P("seq", None)),
        out_specs=(both, both, both, both, P("head", "seq")),
        check_vma=False,
    )
```

```python
import functools
import math

import jax
import jax.numpy as jnp
from jax import lax
from jax.experimental import pallas as pl
from jax.experimental.pallas import tpu as pltpu
from jax.sharding import PartitionSpec as P

HD = 128
TILE = 384
REACH = 2
PARTS = 1
SLOTS = 4
RIM = REACH * TILE
F32 = jnp.float32
BF16 = jnp.bfloat16


def dot_nt(a, b):
    return lax.dot_general(a, b, (((1,), (1,)), ((), ())), preferred_element_type=F32)


def dot_nn(a, b):
    return lax.dot_general(a, b, (((1,), (0,)), ((), ())), preferred_element_type=F32)


def dot_tn(a, b):
    return lax.dot_general(a, b, (((0,), (0,)), ((), ())), preferred_element_type=F32)


def fold(op, x):
    out = x[:, :HD]
    for i in range(1, x.shape[1] // HD):
        out = op(out, x[:, i * HD : (i + 1) * HD])
    return out


def attend(rows, tiles, place, count, q, g, km, vm, far, near, att, dq, mid, rim_far, rim_near, kx, vx, dk, dv, scr):
    t = pl.program_id(1)
    scale = 1.0 / math.sqrt(HD)
    c = scale * math.log2(math.e)
    hi = RIM + rows

    @pl.when(t == 0)
    def _():
        kx[:RIM] = far[0]
        kx[RIM:hi] = km[...]
        kx[hi:] = near[0]
        vx[:RIM] = far[1]
        vx[RIM:hi] = vm[...]
        vx[hi:] = near[1]
        dk[...] = jnp.zeros_like(dk)
        dv[...] = jnp.zeros_like(dv)

    live = count[t]
    qv = q[...]
    gv = g[...]

    def at(j):
        return pl.ds(pl.multiple_of(place[t * SLOTS + j] * TILE, TILE), TILE)

    def slots(step, carry):
        for j in range(SLOTS):
            carry = step(j, carry)
        return carry

    def score(j, m):
        s = dot_nt(qv, kx[at(j), :])
        if j:
            s = jnp.where(j < live, s, -1e30)
        scr[j] = s
        return jnp.maximum(m, fold(jnp.maximum, s))

    m = slots(score, jnp.full((TILE, HD), -3e38, F32))
    m = jnp.max(m, axis=1, keepdims=True)

    def soft(j, carry):
        total, acc = carry
        e = jnp.exp2((scr[j] - m) * c)
        scr[j] = e
        return total + fold(jnp.add, e), acc + dot_nn(e.astype(BF16), vx[at(j), :])

    zero = jnp.zeros((TILE, HD), F32)
    total, acc = slots(soft, (zero, zero))
    inv = 1.0 / jnp.sum(total, axis=1, keepdims=True)
    out = (acc * inv).astype(BF16)
    att[...] = out
    delta = jnp.sum(gv.astype(F32) * out.astype(F32), axis=1, keepdims=True)

    def back(j, acc):
        here = at(j)
        k = kx[here, :]
        p = scr[j] * inv
        ds = (p * (dot_nt(gv, vx[here, :]) - delta)).astype(BF16)
        dv[here, :] += dot_tn(p.astype(BF16), gv)
        dk[here, :] += dot_tn(ds, qv)
        return acc + dot_nn(ds, k)

    dq[...] = (slots(back, zero) * scale).astype(BF16)

    @pl.when(t == tiles - 1)
    def _():
        rim_far[0] = (dk[:RIM] * scale).astype(BF16)
        rim_far[1] = dv[:RIM].astype(BF16)
        mid[0] = dk[RIM:hi] * scale
        mid[1] = dv[RIM:hi]
        rim_near[0] = dk[hi:] * scale
        rim_near[1] = dv[hi:]


def attention_call(place, count, q, g, k, v, far, near, first, heads):
    rows = q.shape[0]
    tiles = rows // TILE
    ext = rows + 2 * RIM
    cols = heads * HD
    tile_in = pl.BlockSpec((TILE, HD), lambda h, t, *_: (t, first + h))
    slab_in = pl.BlockSpec((rows, HD), lambda h, t, *_: (0, first + h))
    rim = pl.BlockSpec((2, RIM, HD), lambda h, t, *_: (0, 0, h))
    tile_out = pl.BlockSpec((TILE, HD), lambda h, t, *_: (t, h))
    mid = pl.BlockSpec((2, rows, HD), lambda h, t, *_: (0, 0, h))
    pairs = heads * tiles * SLOTS
    return pl.pallas_call(
        functools.partial(attend, rows, tiles),
        grid_spec=pltpu.PrefetchScalarGridSpec(
            num_scalar_prefetch=2,
            grid=(heads, tiles),
            in_specs=[tile_in, tile_in, slab_in, slab_in, rim, rim],
            out_specs=[tile_out, tile_out, mid, rim, rim],
            scratch_shapes=[
                pltpu.VMEM((ext, HD), BF16),
                pltpu.VMEM((ext, HD), BF16),
                pltpu.VMEM((ext, HD), F32),
                pltpu.VMEM((ext, HD), F32),
                pltpu.VMEM((SLOTS, TILE, TILE), F32),
            ],
        ),
        out_shape=[
            jax.ShapeDtypeStruct((rows, cols), BF16),
            jax.ShapeDtypeStruct((rows, cols), BF16),
            jax.ShapeDtypeStruct((2, rows, cols), F32),
            jax.ShapeDtypeStruct((2, RIM, cols), BF16),
            jax.ShapeDtypeStruct((2, RIM, cols), F32),
        ],
        compiler_params=pltpu.CompilerParams(
            dimension_semantics=("arbitrary", "arbitrary"), vmem_limit_bytes=40 << 20
        ),
        cost_estimate=pl.CostEstimate(
            flops=pairs * 12 * TILE * TILE * HD,
            bytes_accessed=rows * cols * 40,
            transcendentals=pairs * TILE * TILE,
        ),
    )(place, count, q, g, k, v, far, near)


def swap(x, axis, bit):
    return lax.ppermute(x, axis, [(i, i ^ bit) for i in range(lax.axis_size(axis))])


def shift(x, axis, even_step):
    size = lax.axis_size(axis)
    pairs = [(i, i + (even_step if i % 2 == 0 else -even_step)) for i in range(size)]
    return lax.ppermute(x, axis, [(i, j) for i, j in pairs if 0 <= j < size])


MESH = pl.DeviceIdType.MESH

def mega(
    q_hbm, k_hbm, v_hbm, w_hbm, c_hbm, nb,
    proj_hbm, dq_hbm, dk_hbm, dv_hbm, gw_hbm,
    q, kx, vx, cot, w, g, att, dq, e, scr, st, ak, av,
    far_out, far_in, near_out, near_in, wx_out, wx_in, two_out, two_in, keep, four_out, four_in, gw,
    uz_out, uz_in, u4_out, u4_in, ux_out, ux_in,
    core_out, core_in, y_out, y_in,
    loc_s, out_s, kv_s, kv_r, fw_s, fw_r, cy_s, cy_r, cc_s, cc_r, rf_s, rf_r, rn_s, rn_r,
    wx_s, wx_r, two_s, two_r, four_s, four_r, co_s, co_r, y_s, y_r, u_s, u_r,
    *, seq, norm,
):
    s, h = lax.axis_index("seq"), lax.axis_index("head")
    x, z0, z1 = s % 2, (s // 2) % 2, (s // 4) % 2
    h0, h1 = h % 2, (h // 2) % 2
    beside = (s + 1 - 2 * x, h)
    hop2 = (s + 2 - 4 * z0, h)
    hop4 = (s + 4 - 8 * z1, h)
    mate = (s, h + 1 - 2 * h0)
    across = (s, h + 2 - 4 * h1)
    rows, cols = q.shape
    heads = cols // HD
    tiles = rows // TILE
    width = proj_hbm.shape[1]
    piece = gw_hbm.shape[1]
    scale = 1.0 / math.sqrt(HD)
    c2 = scale * math.log2(math.e)
    up, down = s + 2 - 4 * x, s - 2 + 4 * x
    has_up = (up >= 0) & (up < seq)
    has_down = (down >= 0) & (down < seq)

    def slab(i):
        return pl.ds(pl.multiple_of(i * rows, TILE), rows)

    far_at, near_at, mid_at = slab(2 * x), slab(2 - 2 * x), pl.ds(rows, rows)

    def send(src, dst, sem_s, sem_r, dev):
        return pltpu.make_async_remote_copy(
            src_ref=src, dst_ref=dst, send_sem=sem_s, recv_sem=sem_r,
            device_id=dev, device_id_type=MESH,
        )

    def hcol(i):
        return slice(i * HD, (i + 1) * HD)

    local = [pltpu.make_async_copy(c_hbm, cot.at[0], loc_s.at[0]),
             pltpu.make_async_copy(q_hbm, q, loc_s.at[1]),
             pltpu.make_async_copy(w_hbm, w, loc_s.at[2])]
    for i in range(heads):
        local.append(pltpu.make_async_copy(k_hbm.at[:, hcol(i)], kx.at[i, mid_at], loc_s.at[3 + 2 * i]))
        local.append(pltpu.make_async_copy(v_hbm.at[:, hcol(i)], vx.at[i, mid_at], loc_s.at[4 + 2 * i]))
    for copy in local:
        copy.start()

    @pl.when(jnp.logical_not(has_down))
    def _():
        for i in range(heads):
            kx[i, far_at] = jnp.zeros((rows, HD), BF16)
            vx[i, far_at] = jnp.zeros((rows, HD), BF16)

    barrier = pltpu.get_barrier_semaphore()
    for dev in (beside, hop4, mate, across):
        pl.semaphore_signal(barrier, inc=1, device_id=dev, device_id_type=MESH)

    @pl.when(s >= 2)
    def _():
        pl.semaphore_signal(barrier, inc=1, device_id=(s - 2, h), device_id_type=MESH)

    @pl.when(s + 2 < seq)
    def _():
        pl.semaphore_signal(barrier, inc=1, device_id=(s + 2, h), device_id_type=MESH)

    pl.semaphore_wait(barrier, 4 + (s + seq - 2) // seq + (2 * seq - 3 - s) // seq)

    kv, fw = [], []
    for i in range(heads):
        for n, (src, buf) in enumerate(((k_hbm, kx), (v_hbm, vx))):
            kv.append(send(src.at[:, hcol(i)], buf.at[i, slab(2 * x)], kv_s.at[2 * i + n], kv_r.at[2 * i + n], beside))
            fw.append(send(buf.at[i, near_at], buf.at[i, far_at], fw_s.at[2 * i + n], fw_r.at[2 * i + n], (up, h)))
    tile_rows = [pl.ds(t * TILE, TILE) for t in range(tiles)]
    cy = [send(c_hbm.at[r], cot.at[2, r], cy_s.at[t], cy_r.at[t], across) for t, r in enumerate(tile_rows)]
    cc = [send(cot.at[2, r], cot.at[3, r], cc_s.at[t], cc_r.at[t], mate) for t, r in enumerate(tile_rows)]
    cm = send(c_hbm, cot.at[1], cc_s.at[tiles], cc_r.at[tiles], mate)
    for copy in kv[:2] + cy + [cm] + kv[2:]:
        copy.start()

    def forward_halo(i):
        for n in range(2):
            kv[2 * i + n].wait_recv()

            @pl.when(has_up)
            def _():
                fw[2 * i + n].start()

    def halo(i):
        @pl.when(has_down)
        def _():
            for n in range(2):
                fw[2 * i + n].wait_recv()

    def dead(t, c):
        cand = s * tiles - REACH + t + c
        hit = sum(((nb[t, j] == cand) & (cand >= 0)).astype(jnp.int32) for j in range(SLOTS))
        return (1 - hit).astype(F32) * 1e30

    def tile(t):
        return pl.ds(pl.multiple_of(t * TILE, TILE), TILE)

    def cand(t, c):
        return pl.ds(pl.multiple_of((t + c) * TILE, TILE), TILE)

    spread = 2 * REACH + 1

    def each_tile(step):
        def body(t, carry):
            step(t)
            return carry

        lax.fori_loop(0, tiles, body, 0)

    def fwd(i):
        def step(t):
            at = tile(t)
            qv = q[at, hcol(i)]
            m = jnp.full((8, TILE), -3e38, F32)
            off = [dead(t, c) for c in range(spread)]
            for c in range(spread):
                sc = dot_nt(kx[i, cand(t, c), :], qv)
                scr[0, c] = sc
                m = jnp.maximum(m, jnp.max(sc.reshape(TILE // 8, 8, TILE), axis=0) - off[c])
            m = jnp.max(m, axis=0, keepdims=True) * c2
            total = jnp.zeros((8, TILE), F32)
            acc = jnp.zeros((TILE, HD), F32)
            for c in range(spread):
                p = jnp.exp2(scr[0, c] * c2 - (m + off[c]))
                total = total + jnp.sum(p.reshape(TILE // 8, 8, TILE), axis=0)
                low = p.astype(BF16)
                e[i % 2, t, c] = low
                acc = acc + dot_tn(low, vx[i, cand(t, c), :])
            inv = jnp.broadcast_to(1.0 / jnp.sum(total, axis=0, keepdims=True), (HD, TILE)).T
            att[at, hcol(i)] = (acc * inv).astype(BF16)
            st[i % 2, t] = inv

        each_tile(step)

    def bwd(i):
        ak[i] = jnp.zeros_like(ak[i])
        av[i] = jnp.zeros_like(av[i])

        def step(t):
            at = tile(t)
            qv = q[at, hcol(i)]
            gv = g[at, hcol(i)].astype(F32) * st[i % 2, t]
            delta = jnp.sum((gv * att[at, hcol(i)].astype(F32)).T, axis=0, keepdims=True)
            gb = gv.astype(BF16)
            acc = jnp.zeros((TILE, HD), F32)
            for c in range(spread):
                here = cand(t, c)
                p = e[i % 2, t, c]
                ds = (p.astype(F32) * (dot_nt(vx[i, here, :], gb) - delta)).astype(BF16)
                av[i, here, :] += dot_nn(p, gb)
                ak[i, here, :] += dot_nn(ds, qv)
                acc = acc + dot_tn(ds, kx[i, here, :])
            dq[at, hcol(i)] = (acc * scale).astype(BF16)

        each_tile(step)

    rf = [[send(far_out.at[i, n], far_in.at[i, n], rf_s.at[i, n], rf_r.at[i, n], (down, h)) for n in range(2)]
          for i in range(heads)]
    rn = [[send(near_out.at[i, n], near_in.at[i, n], rn_s.at[i, n], rn_r.at[i, n], beside) for n in range(2)]
          for i in range(heads)]
    part = (lambda i, at: ak[i, at] * scale, lambda i, at: av[i, at])

    def send_far(i):
        @pl.when(has_down)
        def _():
            for n in range(2):
                far_out[i, n] = part[n](i, far_at).astype(BF16)
                rf[i][n].start()

    def relay(i):
        for n in range(2):
            @pl.when(has_up)
            def _():
                rf[i][n].wait_recv()
                near_out[i, n] = (part[n](i, near_at) + far_in[i, n].astype(F32)).astype(BF16)

            @pl.when(jnp.logical_not(has_up))
            def _():
                near_out[i, n] = part[n](i, near_at).astype(BF16)

            rn[i][n].start()

    outs = []

    def write(src, dst):
        copy = pltpu.make_async_copy(src, dst, out_s.at[len(outs)])
        copy.start()
        outs.append(copy)

    def settle(i):
        @pl.when(has_down)
        def _():
            for n in range(2):
                rf[i][n].wait_send()

        for n, dst in enumerate((dk_hbm, dv_hbm)):
            rn[i][n].wait_recv()
            far_out[i, n] = (part[n](i, mid_at) + near_in[i, n].astype(F32)).astype(BF16)
            write(far_out.at[i, n], dst.at[:, hcol(i)])

    def shard(k):
        return (h0 + z0 + k % 2) % 2 + 2 * ((h1 + z1 + k // 2) % 2)

    def term(i, k, side):
        at = pl.ds(pl.multiple_of(side * piece, piece), piece)
        return dot_tn(att[:, hcol(i)], cot[shard(k), :, at])

    rest = heads - 1
    wx = [send(wx_out.at[p], wx_in.at[p], wx_s.at[p], wx_r.at[p], beside) for p in range(rest)]
    twos = [send(two_out.at[p], two_in.at[p], two_s.at[p], two_r.at[p], hop2) for p in range(rest)]
    fours = [send(four_out.at[p], four_in.at[p], four_s.at[p], four_r.at[p], hop4) for p in range(rest)]

    def weight_x(i):
        for k in range(4):
            wx_out[i - 1, k] = term(i, k, 1 - x).astype(BF16)
        wx[i - 1].start()

    def weight_two(i):
        own = [term(i, k, x) for k in range(4)]
        p = i - 1
        wx[p].wait_recv()
        for n, k in enumerate((1, 3)):
            two_out[p, n] = (own[k] + wx_in[p, k].astype(F32)).astype(BF16)
        twos[p].start()
        for n, k in enumerate((0, 2)):
            keep[p, n] = own[k] + wx_in[p, k].astype(F32)

    def weight_four(i):
        p = i - 1
        twos[p].wait_recv()
        four_out[p] = (keep[p, 1] + two_in[p, 1].astype(F32)).astype(BF16)
        fours[p].start()
        keep[p, 0] += two_in[p, 0].astype(F32)

    def weight_done(i):
        p = i - 1
        fours[p].wait_recv()
        gw[hcol(i)] = (keep[p, 0] + four_in[p].astype(F32)) * norm
        write(gw.at[hcol(i)], gw_hbm.at[hcol(i)])

    soon = (h1 + z1) % 2
    uz = [send(uz_out.at[n], uz_in.at[n], u_s.at[j], u_r.at[j], hop2) for j, n in enumerate((soon, 1 - soon))]
    u4 = send(u4_out, u4_in, u_s.at[2], u_r.at[2], hop4)
    ux = send(ux_out, ux_in, u_s.at[3], u_r.at[3], beside)

    def first_two(j):
        n = soon if j == 0 else 1 - soon
        for side in range(2):
            uz_out[n, side] = term(0, 1 + 2 * n, side).astype(BF16)
        uz[j].start()

    def first_four():
        own = [term(0, 2, side) for side in range(2)]
        for j in range(2):
            uz[j].wait_recv()
        for side in range(2):
            u4_out[side] = (own[side] + uz_in[1, side].astype(F32)).astype(BF16)
        u4.start()

    def first_x():
        u4.wait_recv()
        for side, to in ((1 - x, ux_out), (x, gw)):
            total = term(0, 0, side) + uz_in[0, side].astype(F32) + u4_in[side].astype(F32)
            to[:HD] = total.astype(to.dtype)
        ux.start()

    def first_done():
        ux.wait_recv()
        gw[:HD] = (gw[:HD] + ux_in[...].astype(F32)) * norm
        write(gw.at[:HD], gw_hbm.at[:HD])

    def wcols(r):
        b0, b1 = (h0 + r % 2) % 2, (h1 + r // 2) % 2
        return pl.ds(pl.multiple_of((b0 + 2 * b1) * width, width), width)

    def share(t, r):
        return dot_nn(att[tile_rows[t], :], w[:, wcols(r)])

    cores = [[send(core_out.at[n, t], core_in.at[n, t], co_s.at[n, t], co_r.at[n, t], mate) for t in range(tiles)]
             for n in range(2)]
    ys = [send(y_out.at[t], y_in.at[t], y_s.at[t], y_r.at[t], across) for t in range(tiles)]

    def project_out():
        for n, r in enumerate((3, 1)):
            for t in range(tiles):
                core_out[n, t] = share(t, r).astype(BF16)
                cores[n][t].start()
        for t in range(tiles):
            total = share(t, 2)
            cores[0][t].wait_recv()
            y_out[t] = (total + core_in[0, t].astype(F32)).astype(BF16)
            ys[t].start()

    def project_in(t):
        total = share(t, 0)
        cores[1][t].wait_recv()
        ys[t].wait()
        y_out[t] = (total + core_in[1, t].astype(F32) + y_in[t].astype(F32)).astype(BF16)
        write(y_out.at[t], proj_hbm.at[tile_rows[t]])

    def grad_begin(t):
        total = dot_nt(cot[0, tile_rows[t]], w[:, wcols(0)])
        total += dot_nt(cot[1, tile_rows[t]], w[:, wcols(1)])
        for i in range(heads):
            ak[i, tile_rows[t]] = total[:, hcol(i)]

    def grad_end(t):
        total = dot_nt(cot[2, tile_rows[t]], w[:, wcols(2)])
        total += dot_nt(cot[3, tile_rows[t]], w[:, wcols(3)])
        for i in range(heads):
            g[tile_rows[t], hcol(i)] = (ak[i, tile_rows[t]] + total[:, hcol(i)]).astype(BF16)

    forward_halo(0)
    forward_halo(1)
    for copy in local:
        copy.wait()
    halo(0)
    cm.wait_recv()
    cy[0].wait_recv()
    cc[0].start()
    fwd(0)
    first_two(0)
    for t in range(tiles):
        grad_begin(t)
    halo(1)
    fwd(1)
    cy[1].wait_recv()
    cc[1].start()
    forward_halo(2)
    cc[0].wait_recv()
    cc[1].wait_recv()
    for t in range(tiles):
        grad_end(t)
    first_two(1)
    weight_x(1)
    bwd(0)
    send_far(0)
    forward_halo(3)
    halo(2)
    fwd(2)
    first_four()
    weight_x(2)
    bwd(1)
    weight_two(1)
    relay(0)
    halo(3)
    fwd(3)
    send_far(1)
    project_out()
    weight_x(3)
    weight_two(2)
    bwd(3)
    send_far(3)
    relay(1)
    bwd(2)
    send_far(2)
    write(dq, dq_hbm)
    relay(3)
    weight_four(1)
    weight_four(2)
    weight_two(3)
    relay(2)
    for t in range(tiles):
        project_in(t)
    weight_four(3)
    settle(0)
    settle(1)
    settle(3)
    weight_done(1)
    first_x()
    weight_done(2)
    settle(2)
    weight_done(3)
    first_done()

    for copy in outs:
        copy.wait()

    @pl.when(has_up)
    def _():
        for copy in fw:
            copy.wait_send()

    for copy in kv + cy + cc + [cm] + sum(rn, []) + wx + twos + fours + cores[0] + cores[1] + uz + [u4, ux]:
        copy.wait_send()


def mega_call(q, k, v, w, c, nb, seq, norm):
    rows, cols = q.shape
    heads = cols // HD
    tiles = rows // TILE
    width = c.shape[1]
    piece = width * 4 // seq
    rest = heads - 1
    ext = 3 * rows
    spread = 2 * REACH + 1
    hbm = pl.BlockSpec(memory_space=pl.ANY)
    sem = pltpu.SemaphoreType.DMA
    vm = pltpu.VMEM
    return pl.pallas_call(
        functools.partial(mega, seq=seq, norm=norm),
        in_specs=[hbm] * 5 + [pl.BlockSpec(memory_space=pltpu.SMEM)],
        out_specs=[hbm] * 5,
        out_shape=[
            jax.ShapeDtypeStruct((rows, width), BF16),
            jax.ShapeDtypeStruct((rows, cols), BF16),
            jax.ShapeDtypeStruct((rows, cols), BF16),
            jax.ShapeDtypeStruct((rows, cols), BF16),
            jax.ShapeDtypeStruct((cols, piece), F32),
        ],
        scratch_shapes=[
            vm((rows, cols), BF16),
            vm((heads, ext, HD), BF16),
            vm((heads, ext, HD), BF16),
            vm((4, rows, width), BF16),
            vm(w.shape, BF16),
            vm((rows, cols), BF16),
            vm((rows, cols), BF16),
            vm((rows, cols), BF16),
            vm((2, tiles, spread, TILE, TILE), BF16),
            vm((1, spread, TILE, TILE), F32),
            vm((2, tiles, TILE, HD), F32),
            vm((heads, ext, HD), F32),
            vm((heads, ext, HD), F32),
            vm((heads, 2, rows, HD), BF16),
            vm((heads, 2, rows, HD), BF16),
            vm((heads, 2, rows, HD), BF16),
            vm((heads, 2, rows, HD), BF16),
            vm((rest, 4, HD, piece), BF16),
            vm((rest, 4, HD, piece), BF16),
            vm((rest, 2, HD, piece), BF16),
            vm((rest, 2, HD, piece), BF16),
            vm((rest, 2, HD, piece), F32),
            vm((rest, HD, piece), BF16),
            vm((rest, HD, piece), BF16),
            vm((cols, piece), F32),
            vm((2, 2, HD, piece), BF16),
            vm((2, 2, HD, piece), BF16),
            vm((2, HD, piece), BF16),
            vm((2, HD, piece), BF16),
            vm((HD, piece), BF16),
            vm((HD, piece), BF16),
            vm((2, tiles, TILE, width), BF16),
            vm((2, tiles, TILE, width), BF16),
            vm((tiles, TILE, width), BF16),
            vm((tiles, TILE, width), BF16),
            sem((3 + 2 * heads,)), sem((1 + 3 * heads + tiles,)),
            sem((2 * heads,)), sem((2 * heads,)), sem((2 * heads,)), sem((2 * heads,)),
            sem((tiles,)), sem((tiles,)), sem((tiles + 1,)), sem((tiles + 1,)),
            sem((heads, 2)), sem((heads, 2)), sem((heads, 2)), sem((heads, 2)),
            sem((rest,)), sem((rest,)), sem((rest,)), sem((rest,)), sem((rest,)), sem((rest,)),
            sem((2, tiles)), sem((2, tiles)), sem((tiles,)), sem((tiles,)), sem((4,)), sem((4,)),
        ],
        compiler_params=pltpu.CompilerParams(
            collective_id=0, has_side_effects=True, vmem_limit_bytes=62 << 20
        ),
        cost_estimate=pl.CostEstimate(
            flops=16 * rows * cols * width * 3, bytes_accessed=40 << 20, transcendentals=0
        ),
    )(q, k, v, w, c, nb)


def store(n, *refs):
    srcs, dsts, bufs = refs[:n], refs[n : 2 * n], refs[2 * n : 3 * n]
    in_sem, out_sem = refs[3 * n :]
    pairs = []
    for i in range(n):
        step = srcs[i].shape[0] // PARTS
        for j in range(PARTS):
            at = pl.ds(j * step, step)
            pairs.append((
                pltpu.make_async_copy(srcs[i].at[at], bufs[i].at[at], in_sem.at[i, j]),
                pltpu.make_async_copy(bufs[i].at[at], dsts[i].at[at], out_sem.at[i, j]),
            ))
    for load, _ in pairs:
        load.start()
    for load, save in pairs:
        load.wait()
        save.start()
    for _, save in pairs:
        save.wait()


def store_call(arrays):
    hbm = pl.BlockSpec(memory_space=pl.ANY)
    n = len(arrays)
    sems = pltpu.SemaphoreType.DMA((n, PARTS))
    return pl.pallas_call(
        functools.partial(store, n),
        in_specs=[hbm] * n,
        out_specs=[hbm] * n,
        out_shape=[jax.ShapeDtypeStruct(a.shape, a.dtype) for a in arrays],
        scratch_shapes=[pltpu.VMEM(a.shape, a.dtype) for a in arrays] + [sems, sems],
        compiler_params=pltpu.CompilerParams(vmem_limit_bytes=60 << 20),
        cost_estimate=pl.CostEstimate(flops=0, bytes_accessed=8 << 20, transcendentals=0),
    )(*arrays)


def local(queries, key_rows, value_rows, out_weight, cotangent, neighbours):
    rows, columns = queries.shape
    heads = columns // HD
    tiles = rows // TILE
    seq, head = lax.axis_size("seq"), lax.axis_size("head")
    s = lax.axis_index("seq")
    norm = 1.0 / math.sqrt(rows * seq)
    chunks = 2
    per = heads // chunks
    if head == 4 and seq == 8 and heads == 4 and tiles == REACH:
        return store_call(
            mega_call(queries, key_rows, value_rows, out_weight, cotangent, neighbours, seq, norm)
        )

    halos = []
    for n in range(chunks):
        cut = slice(n * per * HD, (n + 1) * per * HD)
        kv = jnp.stack([key_rows[:, cut], value_rows[:, cut]])
        near = swap(kv, "seq", 1)
        far = shift(near, "seq", 2)
        halos.append((far, near))

    full = lax.all_gather(cotangent, "head", axis=1, tiled=True)
    grad_attention = dot_nt(full, out_weight).astype(BF16)

    first = s * tiles - REACH
    alive = neighbours >= 0
    index = jnp.where(alive, neighbours - first, 0)
    span = tiles + REACH
    odd = s % 2 == 1
    turned = jnp.where(index < REACH, index + span, jnp.where(index >= span, index - span, index))
    place = jnp.where(odd, turned, index).reshape(-1).astype(jnp.int32)
    count = jnp.sum(alive, axis=1).astype(jnp.int32)

    atts, dqs, mids, fars, nears = [], [], [], [], []
    for n in range(chunks):
        far, near = halos[n]
        att, dq, mid, rim_far, rim_near = attention_call(
            place, count, queries, grad_attention, key_rows, value_rows, far, near, n * per, per
        )
        atts.append(att)
        dqs.append(dq)
        mids.append(mid)
        fars.append(rim_far)
        nears.append(rim_near)

    grad_queries = jnp.concatenate(dqs, axis=1)
    dks, dvs = [], []
    for n in range(chunks):
        relayed = shift(fars[n], "seq", -2)
        back = swap((nears[n] + relayed.astype(F32)).astype(BF16), "seq", 1)
        done = (mids[n] + back.astype(F32)).astype(BF16)
        dks.append(done[0])
        dvs.append(done[1])
    attention = jnp.concatenate(atts, axis=1)
    projected = lax.psum_scatter(
        dot_nn(attention, out_weight).astype(BF16), "head", scatter_dimension=1, tiled=True
    )
    grad_weight = (
        lax.psum_scatter(
            dot_tn(attention, full).astype(BF16), "seq", scatter_dimension=1, tiled=True
        ).astype(F32)
        * norm
    )
    return (
        projected,
        grad_queries,
        jnp.concatenate(dks, axis=1),
        jnp.concatenate(dvs, axis=1),
        grad_weight,
    )


def solution(mesh):
    both = P("seq", "head")
    return jax.shard_map(
        local,
        mesh=mesh,
        in_specs=(both, both, both, P("head", None), both, P("seq", None)),
        out_specs=(both, both, both, both, P("head", "seq")),
        check_vma=False,
    )
```

```python
import functools
import math

import jax
import jax.numpy as jnp
from jax import lax
from jax.experimental import pallas as pl
from jax.experimental.pallas import tpu as pltpu
from jax.sharding import PartitionSpec as P

HD = 128
TILE = 384
REACH = 2
PARTS = 1
SLOTS = 4
RIM = REACH * TILE
F32 = jnp.float32
BF16 = jnp.bfloat16


def dot_nt(a, b):
    return lax.dot_general(a, b, (((1,), (1,)), ((), ())), preferred_element_type=F32)


def dot_nn(a, b):
    return lax.dot_general(a, b, (((1,), (0,)), ((), ())), preferred_element_type=F32)


def dot_tn(a, b):
    return lax.dot_general(a, b, (((0,), (0,)), ((), ())), preferred_element_type=F32)


def fold(op, x):
    out = x[:, :HD]
    for i in range(1, x.shape[1] // HD):
        out = op(out, x[:, i * HD : (i + 1) * HD])
    return out


def attend(rows, tiles, place, count, q, g, km, vm, far, near, att, dq, mid, rim_far, rim_near, kx, vx, dk, dv, scr):
    t = pl.program_id(1)
    scale = 1.0 / math.sqrt(HD)
    c = scale * math.log2(math.e)
    hi = RIM + rows

    @pl.when(t == 0)
    def _():
        kx[:RIM] = far[0]
        kx[RIM:hi] = km[...]
        kx[hi:] = near[0]
        vx[:RIM] = far[1]
        vx[RIM:hi] = vm[...]
        vx[hi:] = near[1]
        dk[...] = jnp.zeros_like(dk)
        dv[...] = jnp.zeros_like(dv)

    live = count[t]
    qv = q[...]
    gv = g[...]

    def at(j):
        return pl.ds(pl.multiple_of(place[t * SLOTS + j] * TILE, TILE), TILE)

    def slots(step, carry):
        for j in range(SLOTS):
            carry = step(j, carry)
        return carry

    def score(j, m):
        s = dot_nt(qv, kx[at(j), :])
        if j:
            s = jnp.where(j < live, s, -1e30)
        scr[j] = s
        return jnp.maximum(m, fold(jnp.maximum, s))

    m = slots(score, jnp.full((TILE, HD), -3e38, F32))
    m = jnp.max(m, axis=1, keepdims=True)

    def soft(j, carry):
        total, acc = carry
        e = jnp.exp2((scr[j] - m) * c)
        scr[j] = e
        return total + fold(jnp.add, e), acc + dot_nn(e.astype(BF16), vx[at(j), :])

    zero = jnp.zeros((TILE, HD), F32)
    total, acc = slots(soft, (zero, zero))
    inv = 1.0 / jnp.sum(total, axis=1, keepdims=True)
    out = (acc * inv).astype(BF16)
    att[...] = out
    delta = jnp.sum(gv.astype(F32) * out.astype(F32), axis=1, keepdims=True)

    def back(j, acc):
        here = at(j)
        k = kx[here, :]
        p = scr[j] * inv
        ds = (p * (dot_nt(gv, vx[here, :]) - delta)).astype(BF16)
        dv[here, :] += dot_tn(p.astype(BF16), gv)
        dk[here, :] += dot_tn(ds, qv)
        return acc + dot_nn(ds, k)

    dq[...] = (slots(back, zero) * scale).astype(BF16)

    @pl.when(t == tiles - 1)
    def _():
        rim_far[0] = (dk[:RIM] * scale).astype(BF16)
        rim_far[1] = dv[:RIM].astype(BF16)
        mid[0] = dk[RIM:hi] * scale
        mid[1] = dv[RIM:hi]
        rim_near[0] = dk[hi:] * scale
        rim_near[1] = dv[hi:]


def attention_call(place, count, q, g, k, v, far, near, first, heads):
    rows = q.shape[0]
    tiles = rows // TILE
    ext = rows + 2 * RIM
    cols = heads * HD
    tile_in = pl.BlockSpec((TILE, HD), lambda h, t, *_: (t, first + h))
    slab_in = pl.BlockSpec((rows, HD), lambda h, t, *_: (0, first + h))
    rim = pl.BlockSpec((2, RIM, HD), lambda h, t, *_: (0, 0, h))
    tile_out = pl.BlockSpec((TILE, HD), lambda h, t, *_: (t, h))
    mid = pl.BlockSpec((2, rows, HD), lambda h, t, *_: (0, 0, h))
    pairs = heads * tiles * SLOTS
    return pl.pallas_call(
        functools.partial(attend, rows, tiles),
        grid_spec=pltpu.PrefetchScalarGridSpec(
            num_scalar_prefetch=2,
            grid=(heads, tiles),
            in_specs=[tile_in, tile_in, slab_in, slab_in, rim, rim],
            out_specs=[tile_out, tile_out, mid, rim, rim],
            scratch_shapes=[
                pltpu.VMEM((ext, HD), BF16),
                pltpu.VMEM((ext, HD), BF16),
                pltpu.VMEM((ext, HD), F32),
                pltpu.VMEM((ext, HD), F32),
                pltpu.VMEM((SLOTS, TILE, TILE), F32),
            ],
        ),
        out_shape=[
            jax.ShapeDtypeStruct((rows, cols), BF16),
            jax.ShapeDtypeStruct((rows, cols), BF16),
            jax.ShapeDtypeStruct((2, rows, cols), F32),
            jax.ShapeDtypeStruct((2, RIM, cols), BF16),
            jax.ShapeDtypeStruct((2, RIM, cols), F32),
        ],
        compiler_params=pltpu.CompilerParams(
            dimension_semantics=("arbitrary", "arbitrary"), vmem_limit_bytes=40 << 20
        ),
        cost_estimate=pl.CostEstimate(
            flops=pairs * 12 * TILE * TILE * HD,
            bytes_accessed=rows * cols * 40,
            transcendentals=pairs * TILE * TILE,
        ),
    )(place, count, q, g, k, v, far, near)


def swap(x, axis, bit):
    return lax.ppermute(x, axis, [(i, i ^ bit) for i in range(lax.axis_size(axis))])


def shift(x, axis, even_step):
    size = lax.axis_size(axis)
    pairs = [(i, i + (even_step if i % 2 == 0 else -even_step)) for i in range(size)]
    return lax.ppermute(x, axis, [(i, j) for i, j in pairs if 0 <= j < size])


MESH = pl.DeviceIdType.MESH

def mega(
    q_hbm, k_hbm, v_hbm, w_hbm, c_hbm, nb,
    proj_hbm, dq_hbm, dk_hbm, dv_hbm, gw_hbm,
    q, kx, vx, cot, w, g, att, dq, e, scr, st, ak, av,
    far_out, far_in, near_out, near_in, wx_out, wx_in, two_out, two_in, keep, four_out, four_in, gw,
    uz_out, uz_in, u4_out, u4_in, ux_out, ux_in,
    core_out, core_in, y_out, y_in,
    loc_s, out_s, kv_s, kv_r, fw_s, fw_r, cy_s, cy_r, cc_s, cc_r, rf_s, rf_r, rn_s, rn_r,
    wx_s, wx_r, two_s, two_r, four_s, four_r, co_s, co_r, y_s, y_r, u_s, u_r,
    *, seq, norm,
):
    s, h = lax.axis_index("seq"), lax.axis_index("head")
    x, z0, z1 = s % 2, (s // 2) % 2, (s // 4) % 2
    h0, h1 = h % 2, (h // 2) % 2
    beside = (s + 1 - 2 * x, h)
    hop2 = (s + 2 - 4 * z0, h)
    hop4 = (s + 4 - 8 * z1, h)
    mate = (s, h + 1 - 2 * h0)
    across = (s, h + 2 - 4 * h1)
    rows, cols = q.shape
    heads = cols // HD
    tiles = rows // TILE
    width = proj_hbm.shape[1]
    piece = gw_hbm.shape[1]
    scale = 1.0 / math.sqrt(HD)
    c2 = scale * math.log2(math.e)
    up, down = s + 2 - 4 * x, s - 2 + 4 * x
    has_up = (up >= 0) & (up < seq)
    has_down = (down >= 0) & (down < seq)

    def slab(i):
        return pl.ds(pl.multiple_of(i * rows, TILE), rows)

    far_at, near_at, mid_at = slab(2 * x), slab(2 - 2 * x), pl.ds(rows, rows)

    def send(src, dst, sem_s, sem_r, dev):
        return pltpu.make_async_remote_copy(
            src_ref=src, dst_ref=dst, send_sem=sem_s, recv_sem=sem_r,
            device_id=dev, device_id_type=MESH,
        )

    def hcol(i):
        return slice(i * HD, (i + 1) * HD)

    local = [pltpu.make_async_copy(c_hbm, cot.at[0], loc_s.at[0]),
             pltpu.make_async_copy(q_hbm, q, loc_s.at[1]),
             pltpu.make_async_copy(w_hbm, w, loc_s.at[2])]
    for i in range(heads):
        local.append(pltpu.make_async_copy(k_hbm.at[:, hcol(i)], kx.at[i, mid_at], loc_s.at[3 + 2 * i]))
        local.append(pltpu.make_async_copy(v_hbm.at[:, hcol(i)], vx.at[i, mid_at], loc_s.at[4 + 2 * i]))
    for copy in local:
        copy.start()

    @pl.when(jnp.logical_not(has_down))
    def _():
        for i in range(heads):
            kx[i, far_at] = jnp.zeros((rows, HD), BF16)
            vx[i, far_at] = jnp.zeros((rows, HD), BF16)

    barrier = pltpu.get_barrier_semaphore()
    for dev in (beside, hop4, mate, across):
        pl.semaphore_signal(barrier, inc=1, device_id=dev, device_id_type=MESH)

    @pl.when(s >= 2)
    def _():
        pl.semaphore_signal(barrier, inc=1, device_id=(s - 2, h), device_id_type=MESH)

    @pl.when(s + 2 < seq)
    def _():
        pl.semaphore_signal(barrier, inc=1, device_id=(s + 2, h), device_id_type=MESH)

    pl.semaphore_wait(barrier, 4 + (s + seq - 2) // seq + (2 * seq - 3 - s) // seq)

    kv, fw = [], []
    for i in range(heads):
        for n, (src, buf) in enumerate(((k_hbm, kx), (v_hbm, vx))):
            kv.append(send(src.at[:, hcol(i)], buf.at[i, slab(2 * x)], kv_s.at[2 * i + n], kv_r.at[2 * i + n], beside))
            fw.append(send(buf.at[i, near_at], buf.at[i, far_at], fw_s.at[2 * i + n], fw_r.at[2 * i + n], (up, h)))
    tile_rows = [pl.ds(t * TILE, TILE) for t in range(tiles)]
    cy = [send(c_hbm.at[r], cot.at[2, r], cy_s.at[t], cy_r.at[t], across) for t, r in enumerate(tile_rows)]
    cc = [send(cot.at[2, r], cot.at[3, r], cc_s.at[t], cc_r.at[t], mate) for t, r in enumerate(tile_rows)]
    cm = send(c_hbm, cot.at[1], cc_s.at[tiles], cc_r.at[tiles], mate)
    for copy in kv[:2] + cy + [cm] + kv[2:]:
        copy.start()

    def forward_halo(i):
        for n in range(2):
            kv[2 * i + n].wait_recv()

            @pl.when(has_up)
            def _():
                fw[2 * i + n].start()

    def halo(i):
        @pl.when(has_down)
        def _():
            for n in range(2):
                fw[2 * i + n].wait_recv()

    def dead(t, c):
        cand = s * tiles - REACH + t + c
        hit = sum(((nb[t, j] == cand) & (cand >= 0)).astype(jnp.int32) for j in range(SLOTS))
        return (1 - hit).astype(F32) * 1e30

    def tile(t):
        return pl.ds(pl.multiple_of(t * TILE, TILE), TILE)

    def cand(t, c):
        return pl.ds(pl.multiple_of((t + c) * TILE, TILE), TILE)

    spread = 2 * REACH + 1

    def each_tile(step):
        def body(t, carry):
            step(t)
            return carry

        lax.fori_loop(0, tiles, body, 0)

    def fwd(i):
        def step(t):
            at = tile(t)
            qv = q[at, hcol(i)]
            m = jnp.full((8, TILE), -3e38, F32)
            off = [dead(t, c) for c in range(spread)]
            for c in range(spread):
                sc = dot_nt(kx[i, cand(t, c), :], qv)
                scr[0, c] = sc
                m = jnp.maximum(m, jnp.max(sc.reshape(TILE // 8, 8, TILE), axis=0) - off[c])
            m = jnp.max(m, axis=0, keepdims=True) * c2
            total = jnp.zeros((8, TILE), F32)
            acc = jnp.zeros((TILE, HD), F32)
            for c in range(spread):
                p = jnp.exp2(scr[0, c] * c2 - (m + off[c]))
                total = total + jnp.sum(p.reshape(TILE // 8, 8, TILE), axis=0)
                low = p.astype(BF16)
                e[i % 2, t, c] = low
                acc = acc + dot_tn(low, vx[i, cand(t, c), :])
            inv = jnp.broadcast_to(1.0 / jnp.sum(total, axis=0, keepdims=True), (HD, TILE)).T
            att[at, hcol(i)] = (acc * inv).astype(BF16)
            st[i % 2, t] = inv

        each_tile(step)

    def bwd(i):
        ak[i] = jnp.zeros_like(ak[i])
        av[i] = jnp.zeros_like(av[i])

        def step(t):
            at = tile(t)
            qv = q[at, hcol(i)]
            gv = g[at, hcol(i)].astype(F32) * st[i % 2, t]
            delta = jnp.sum((gv * att[at, hcol(i)].astype(F32)).T, axis=0, keepdims=True)
            gb = gv.astype(BF16)
            acc = jnp.zeros((TILE, HD), F32)
            for c in range(spread):
                here = cand(t, c)
                p = e[i % 2, t, c]
                ds = (p.astype(F32) * (dot_nt(vx[i, here, :], gb) - delta)).astype(BF16)
                av[i, here, :] += dot_nn(p, gb)
                ak[i, here, :] += dot_nn(ds, qv)
                acc = acc + dot_tn(ds, kx[i, here, :])
            dq[at, hcol(i)] = (acc * scale).astype(BF16)

        each_tile(step)

    rf = [[send(far_out.at[i, n], far_in.at[i, n], rf_s.at[i, n], rf_r.at[i, n], (down, h)) for n in range(2)]
          for i in range(heads)]
    rn = [[send(near_out.at[i, n], near_in.at[i, n], rn_s.at[i, n], rn_r.at[i, n], beside) for n in range(2)]
          for i in range(heads)]
    part = (lambda i, at: ak[i, at] * scale, lambda i, at: av[i, at])

    def send_far(i):
        @pl.when(has_down)
        def _():
            for n in range(2):
                far_out[i, n] = part[n](i, far_at).astype(BF16)
                rf[i][n].start()

    def relay(i):
        for n in range(2):
            @pl.when(has_up)
            def _():
                rf[i][n].wait_recv()
                near_out[i, n] = (part[n](i, near_at) + far_in[i, n].astype(F32)).astype(BF16)

            @pl.when(jnp.logical_not(has_up))
            def _():
                near_out[i, n] = part[n](i, near_at).astype(BF16)

            rn[i][n].start()

    outs = []

    def write(src, dst):
        copy = pltpu.make_async_copy(src, dst, out_s.at[len(outs)])
        copy.start()
        outs.append(copy)

    def settle(i):
        @pl.when(has_down)
        def _():
            for n in range(2):
                rf[i][n].wait_send()

        for n, dst in enumerate((dk_hbm, dv_hbm)):
            rn[i][n].wait_recv()
            far_out[i, n] = (part[n](i, mid_at) + near_in[i, n].astype(F32)).astype(BF16)
            write(far_out.at[i, n], dst.at[:, hcol(i)])

    def shard(k):
        return (h0 + z0 + k % 2) % 2 + 2 * ((h1 + z1 + k // 2) % 2)

    def term(i, k, side):
        at = pl.ds(pl.multiple_of(side * piece, piece), piece)
        return dot_tn(att[:, hcol(i)], cot[shard(k), :, at])

    rest = heads - 1
    wx = [send(wx_out.at[p], wx_in.at[p], wx_s.at[p], wx_r.at[p], beside) for p in range(rest)]
    twos = [send(two_out.at[p], two_in.at[p], two_s.at[p], two_r.at[p], hop2) for p in range(rest)]
    fours = [send(four_out.at[p], four_in.at[p], four_s.at[p], four_r.at[p], hop4) for p in range(rest)]

    def weight_x(i):
        for k in range(4):
            wx_out[i - 1, k] = term(i, k, 1 - x).astype(BF16)
        wx[i - 1].start()

    def weight_two(i):
        own = [term(i, k, x) for k in range(4)]
        p = i - 1
        wx[p].wait_recv()
        for n, k in enumerate((1, 3)):
            two_out[p, n] = (own[k] + wx_in[p, k].astype(F32)).astype(BF16)
        twos[p].start()
        for n, k in enumerate((0, 2)):
            keep[p, n] = own[k] + wx_in[p, k].astype(F32)

    def weight_four(i):
        p = i - 1
        twos[p].wait_recv()
        four_out[p] = (keep[p, 1] + two_in[p, 1].astype(F32)).astype(BF16)
        fours[p].start()
        keep[p, 0] += two_in[p, 0].astype(F32)

    def weight_done(i):
        p = i - 1
        fours[p].wait_recv()
        gw[hcol(i)] = (keep[p, 0] + four_in[p].astype(F32)) * norm
        write(gw.at[hcol(i)], gw_hbm.at[hcol(i)])

    soon = (h1 + z1) % 2
    uz = [send(uz_out.at[n], uz_in.at[n], u_s.at[j], u_r.at[j], hop2) for j, n in enumerate((soon, 1 - soon))]
    u4 = send(u4_out, u4_in, u_s.at[2], u_r.at[2], hop4)
    ux = send(ux_out, ux_in, u_s.at[3], u_r.at[3], beside)

    def first_two(j):
        n = soon if j == 0 else 1 - soon
        for side in range(2):
            uz_out[n, side] = term(0, 1 + 2 * n, side).astype(BF16)
        uz[j].start()

    def first_four():
        own = [term(0, 2, side) for side in range(2)]
        for j in range(2):
            uz[j].wait_recv()
        for side in range(2):
            u4_out[side] = (own[side] + uz_in[1, side].astype(F32)).astype(BF16)
        u4.start()

    def first_x():
        u4.wait_recv()
        for side, to in ((1 - x, ux_out), (x, gw)):
            total = term(0, 0, side) + uz_in[0, side].astype(F32) + u4_in[side].astype(F32)
            to[:HD] = total.astype(to.dtype)
        ux.start()

    def first_done():
        ux.wait_recv()
        gw[:HD] = (gw[:HD] + ux_in[...].astype(F32)) * norm
        write(gw.at[:HD], gw_hbm.at[:HD])

    def wcols(r):
        b0, b1 = (h0 + r % 2) % 2, (h1 + r // 2) % 2
        return pl.ds(pl.multiple_of((b0 + 2 * b1) * width, width), width)

    def share(t, r):
        return dot_nn(att[tile_rows[t], :], w[:, wcols(r)])

    cores = [[send(core_out.at[n, t], core_in.at[n, t], co_s.at[n, t], co_r.at[n, t], mate) for t in range(tiles)]
             for n in range(2)]
    ys = [send(y_out.at[t], y_in.at[t], y_s.at[t], y_r.at[t], across) for t in range(tiles)]

    def project_out():
        for n, r in enumerate((3, 1)):
            for t in range(tiles):
                core_out[n, t] = share(t, r).astype(BF16)
                cores[n][t].start()
        for t in range(tiles):
            total = share(t, 2)
            cores[0][t].wait_recv()
            y_out[t] = (total + core_in[0, t].astype(F32)).astype(BF16)
            ys[t].start()

    def project_in(t):
        total = share(t, 0)
        cores[1][t].wait_recv()
        ys[t].wait()
        y_out[t] = (total + core_in[1, t].astype(F32) + y_in[t].astype(F32)).astype(BF16)
        write(y_out.at[t], proj_hbm.at[tile_rows[t]])

    def grad_begin(t):
        total = dot_nt(cot[0, tile_rows[t]], w[:, wcols(0)])
        total += dot_nt(cot[1, tile_rows[t]], w[:, wcols(1)])
        for i in range(heads):
            ak[i, tile_rows[t]] = total[:, hcol(i)]

    def grad_end(t):
        total = dot_nt(cot[2, tile_rows[t]], w[:, wcols(2)])
        total += dot_nt(cot[3, tile_rows[t]], w[:, wcols(3)])
        for i in range(heads):
            g[tile_rows[t], hcol(i)] = (ak[i, tile_rows[t]] + total[:, hcol(i)]).astype(BF16)

    forward_halo(0)
    for copy in local:
        copy.wait()
    cm.wait_recv()
    forward_halo(1)
    halo(0)
    cy[0].wait_recv()
    cc[0].start()
    for t in range(tiles):
        grad_begin(t)
    fwd(0)
    first_two(0)
    forward_halo(2)
    cy[1].wait_recv()
    cc[1].start()
    halo(1)
    fwd(1)
    cc[0].wait_recv()
    cc[1].wait_recv()
    for t in range(tiles):
        grad_end(t)
    weight_x(1)
    first_two(1)
    bwd(0)
    forward_halo(3)
    send_far(0)
    halo(2)
    fwd(2)
    bwd(1)
    relay(0)
    send_far(1)
    halo(3)
    fwd(3)
    weight_x(3)
    first_four()
    weight_two(1)
    weight_x(2)
    bwd(3)
    send_far(3)
    project_out()
    settle(0)
    relay(1)
    weight_two(2)
    weight_four(1)
    bwd(2)
    send_far(2)
    write(dq, dq_hbm)
    weight_two(3)
    relay(3)
    weight_four(2)
    relay(2)
    settle(1)
    weight_four(3)
    first_x()
    settle(3)
    for t in range(tiles):
        project_in(t)
    settle(2)
    weight_done(2)
    weight_done(3)
    weight_done(1)
    first_done()

    for copy in outs:
        copy.wait()

    @pl.when(has_up)
    def _():
        for copy in fw:
            copy.wait_send()

    for copy in kv + cy + cc + [cm] + sum(rn, []) + wx + twos + fours + cores[0] + cores[1] + uz + [u4, ux]:
        copy.wait_send()


def mega_call(q, k, v, w, c, nb, seq, norm):
    rows, cols = q.shape
    heads = cols // HD
    tiles = rows // TILE
    width = c.shape[1]
    piece = width * 4 // seq
    rest = heads - 1
    ext = 3 * rows
    spread = 2 * REACH + 1
    hbm = pl.BlockSpec(memory_space=pl.ANY)
    sem = pltpu.SemaphoreType.DMA
    vm = pltpu.VMEM
    return pl.pallas_call(
        functools.partial(mega, seq=seq, norm=norm),
        in_specs=[hbm] * 5 + [pl.BlockSpec(memory_space=pltpu.SMEM)],
        out_specs=[hbm] * 5,
        out_shape=[
            jax.ShapeDtypeStruct((rows, width), BF16),
            jax.ShapeDtypeStruct((rows, cols), BF16),
            jax.ShapeDtypeStruct((rows, cols), BF16),
            jax.ShapeDtypeStruct((rows, cols), BF16),
            jax.ShapeDtypeStruct((cols, piece), F32),
        ],
        scratch_shapes=[
            vm((rows, cols), BF16),
            vm((heads, ext, HD), BF16),
            vm((heads, ext, HD), BF16),
            vm((4, rows, width), BF16),
            vm(w.shape, BF16),
            vm((rows, cols), BF16),
            vm((rows, cols), BF16),
            vm((rows, cols), BF16),
            vm((2, tiles, spread, TILE, TILE), BF16),
            vm((1, spread, TILE, TILE), F32),
            vm((2, tiles, TILE, HD), F32),
            vm((heads, ext, HD), F32),
            vm((heads, ext, HD), F32),
            vm((heads, 2, rows, HD), BF16),
            vm((heads, 2, rows, HD), BF16),
            vm((heads, 2, rows, HD), BF16),
            vm((heads, 2, rows, HD), BF16),
            vm((rest, 4, HD, piece), BF16),
            vm((rest, 4, HD, piece), BF16),
            vm((rest, 2, HD, piece), BF16),
            vm((rest, 2, HD, piece), BF16),
            vm((rest, 2, HD, piece), F32),
            vm((rest, HD, piece), BF16),
            vm((rest, HD, piece), BF16),
            vm((cols, piece), F32),
            vm((2, 2, HD, piece), BF16),
            vm((2, 2, HD, piece), BF16),
            vm((2, HD, piece), BF16),
            vm((2, HD, piece), BF16),
            vm((HD, piece), BF16),
            vm((HD, piece), BF16),
            vm((2, tiles, TILE, width), BF16),
            vm((2, tiles, TILE, width), BF16),
            vm((tiles, TILE, width), BF16),
            vm((tiles, TILE, width), BF16),
            sem((3 + 2 * heads,)), sem((1 + 3 * heads + tiles,)),
            sem((2 * heads,)), sem((2 * heads,)), sem((2 * heads,)), sem((2 * heads,)),
            sem((tiles,)), sem((tiles,)), sem((tiles + 1,)), sem((tiles + 1,)),
            sem((heads, 2)), sem((heads, 2)), sem((heads, 2)), sem((heads, 2)),
            sem((rest,)), sem((rest,)), sem((rest,)), sem((rest,)), sem((rest,)), sem((rest,)),
            sem((2, tiles)), sem((2, tiles)), sem((tiles,)), sem((tiles,)), sem((4,)), sem((4,)),
        ],
        compiler_params=pltpu.CompilerParams(
            collective_id=0, has_side_effects=True, vmem_limit_bytes=62 << 20
        ),
        cost_estimate=pl.CostEstimate(
            flops=16 * rows * cols * width * 3, bytes_accessed=40 << 20, transcendentals=0
        ),
    )(q, k, v, w, c, nb)


def store(n, *refs):
    srcs, dsts, bufs = refs[:n], refs[n : 2 * n], refs[2 * n : 3 * n]
    in_sem, out_sem = refs[3 * n :]
    pairs = []
    for i in range(n):
        step = srcs[i].shape[0] // PARTS
        for j in range(PARTS):
            at = pl.ds(j * step, step)
            pairs.append((
                pltpu.make_async_copy(srcs[i].at[at], bufs[i].at[at], in_sem.at[i, j]),
                pltpu.make_async_copy(bufs[i].at[at], dsts[i].at[at], out_sem.at[i, j]),
            ))
    for load, _ in pairs:
        load.start()
    for load, save in pairs:
        load.wait()
        save.start()
    for _, save in pairs:
        save.wait()


def store_call(arrays):
    hbm = pl.BlockSpec(memory_space=pl.ANY)
    n = len(arrays)
    sems = pltpu.SemaphoreType.DMA((n, PARTS))
    return pl.pallas_call(
        functools.partial(store, n),
        in_specs=[hbm] * n,
        out_specs=[hbm] * n,
        out_shape=[jax.ShapeDtypeStruct(a.shape, a.dtype) for a in arrays],
        scratch_shapes=[pltpu.VMEM(a.shape, a.dtype) for a in arrays] + [sems, sems],
        compiler_params=pltpu.CompilerParams(vmem_limit_bytes=60 << 20),
        cost_estimate=pl.CostEstimate(flops=0, bytes_accessed=8 << 20, transcendentals=0),
    )(*arrays)


def local(queries, key_rows, value_rows, out_weight, cotangent, neighbours):
    rows, columns = queries.shape
    heads = columns // HD
    tiles = rows // TILE
    seq, head = lax.axis_size("seq"), lax.axis_size("head")
    s = lax.axis_index("seq")
    norm = 1.0 / math.sqrt(rows * seq)
    chunks = 2
    per = heads // chunks
    if head == 4 and seq == 8 and heads == 4 and tiles == REACH:
        return store_call(
            mega_call(queries, key_rows, value_rows, out_weight, cotangent, neighbours, seq, norm)
        )

    halos = []
    for n in range(chunks):
        cut = slice(n * per * HD, (n + 1) * per * HD)
        kv = jnp.stack([key_rows[:, cut], value_rows[:, cut]])
        near = swap(kv, "seq", 1)
        far = shift(near, "seq", 2)
        halos.append((far, near))

    full = lax.all_gather(cotangent, "head", axis=1, tiled=True)
    grad_attention = dot_nt(full, out_weight).astype(BF16)

    first = s * tiles - REACH
    alive = neighbours >= 0
    index = jnp.where(alive, neighbours - first, 0)
    span = tiles + REACH
    odd = s % 2 == 1
    turned = jnp.where(index < REACH, index + span, jnp.where(index >= span, index - span, index))
    place = jnp.where(odd, turned, index).reshape(-1).astype(jnp.int32)
    count = jnp.sum(alive, axis=1).astype(jnp.int32)

    atts, dqs, mids, fars, nears = [], [], [], [], []
    for n in range(chunks):
        far, near = halos[n]
        att, dq, mid, rim_far, rim_near = attention_call(
            place, count, queries, grad_attention, key_rows, value_rows, far, near, n * per, per
        )
        atts.append(att)
        dqs.append(dq)
        mids.append(mid)
        fars.append(rim_far)
        nears.append(rim_near)

    grad_queries = jnp.concatenate(dqs, axis=1)
    dks, dvs = [], []
    for n in range(chunks):
        relayed = shift(fars[n], "seq", -2)
        back = swap((nears[n] + relayed.astype(F32)).astype(BF16), "seq", 1)
        done = (mids[n] + back.astype(F32)).astype(BF16)
        dks.append(done[0])
        dvs.append(done[1])
    attention = jnp.concatenate(atts, axis=1)
    projected = lax.psum_scatter(
        dot_nn(attention, out_weight).astype(BF16), "head", scatter_dimension=1, tiled=True
    )
    grad_weight = (
        lax.psum_scatter(
            dot_tn(attention, full).astype(BF16), "seq", scatter_dimension=1, tiled=True
        ).astype(F32)
        * norm
    )
    return (
        projected,
        grad_queries,
        jnp.concatenate(dks, axis=1),
        jnp.concatenate(dvs, axis=1),
        grad_weight,
    )


def solution(mesh):
    both = P("seq", "head")
    return jax.shard_map(
        local,
        mesh=mesh,
        in_specs=(both, both, both, P("head", None), both, P("seq", None)),
        out_specs=(both, both, both, both, P("head", "seq")),
        check_vma=False,
    )
```

```python
import functools
import math

import jax
import jax.numpy as jnp
from jax import lax
from jax.experimental import pallas as pl
from jax.experimental.pallas import tpu as pltpu
from jax.sharding import PartitionSpec as P

HD = 128
TILE = 384
REACH = 2
PARTS = 1
SLOTS = 4
RIM = REACH * TILE
F32 = jnp.float32
BF16 = jnp.bfloat16


def dot_nt(a, b):
    return lax.dot_general(a, b, (((1,), (1,)), ((), ())), preferred_element_type=F32)


def dot_nn(a, b):
    return lax.dot_general(a, b, (((1,), (0,)), ((), ())), preferred_element_type=F32)


def dot_tn(a, b):
    return lax.dot_general(a, b, (((0,), (0,)), ((), ())), preferred_element_type=F32)


def fold(op, x):
    out = x[:, :HD]
    for i in range(1, x.shape[1] // HD):
        out = op(out, x[:, i * HD : (i + 1) * HD])
    return out


def attend(rows, tiles, place, count, q, g, km, vm, far, near, att, dq, mid, rim_far, rim_near, kx, vx, dk, dv, scr):
    t = pl.program_id(1)
    scale = 1.0 / math.sqrt(HD)
    c = scale * math.log2(math.e)
    hi = RIM + rows

    @pl.when(t == 0)
    def _():
        kx[:RIM] = far[0]
        kx[RIM:hi] = km[...]
        kx[hi:] = near[0]
        vx[:RIM] = far[1]
        vx[RIM:hi] = vm[...]
        vx[hi:] = near[1]
        dk[...] = jnp.zeros_like(dk)
        dv[...] = jnp.zeros_like(dv)

    live = count[t]
    qv = q[...]
    gv = g[...]

    def at(j):
        return pl.ds(pl.multiple_of(place[t * SLOTS + j] * TILE, TILE), TILE)

    def slots(step, carry):
        for j in range(SLOTS):
            carry = step(j, carry)
        return carry

    def score(j, m):
        s = dot_nt(qv, kx[at(j), :])
        if j:
            s = jnp.where(j < live, s, -1e30)
        scr[j] = s
        return jnp.maximum(m, fold(jnp.maximum, s))

    m = slots(score, jnp.full((TILE, HD), -3e38, F32))
    m = jnp.max(m, axis=1, keepdims=True)

    def soft(j, carry):
        total, acc = carry
        e = jnp.exp2((scr[j] - m) * c)
        scr[j] = e
        return total + fold(jnp.add, e), acc + dot_nn(e.astype(BF16), vx[at(j), :])

    zero = jnp.zeros((TILE, HD), F32)
    total, acc = slots(soft, (zero, zero))
    inv = 1.0 / jnp.sum(total, axis=1, keepdims=True)
    out = (acc * inv).astype(BF16)
    att[...] = out
    delta = jnp.sum(gv.astype(F32) * out.astype(F32), axis=1, keepdims=True)

    def back(j, acc):
        here = at(j)
        k = kx[here, :]
        p = scr[j] * inv
        ds = (p * (dot_nt(gv, vx[here, :]) - delta)).astype(BF16)
        dv[here, :] += dot_tn(p.astype(BF16), gv)
        dk[here, :] += dot_tn(ds, qv)
        return acc + dot_nn(ds, k)

    dq[...] = (slots(back, zero) * scale).astype(BF16)

    @pl.when(t == tiles - 1)
    def _():
        rim_far[0] = (dk[:RIM] * scale).astype(BF16)
        rim_far[1] = dv[:RIM].astype(BF16)
        mid[0] = dk[RIM:hi] * scale
        mid[1] = dv[RIM:hi]
        rim_near[0] = dk[hi:] * scale
        rim_near[1] = dv[hi:]


def attention_call(place, count, q, g, k, v, far, near, first, heads):
    rows = q.shape[0]
    tiles = rows // TILE
    ext = rows + 2 * RIM
    cols = heads * HD
    tile_in = pl.BlockSpec((TILE, HD), lambda h, t, *_: (t, first + h))
    slab_in = pl.BlockSpec((rows, HD), lambda h, t, *_: (0, first + h))
    rim = pl.BlockSpec((2, RIM, HD), lambda h, t, *_: (0, 0, h))
    tile_out = pl.BlockSpec((TILE, HD), lambda h, t, *_: (t, h))
    mid = pl.BlockSpec((2, rows, HD), lambda h, t, *_: (0, 0, h))
    pairs = heads * tiles * SLOTS
    return pl.pallas_call(
        functools.partial(attend, rows, tiles),
        grid_spec=pltpu.PrefetchScalarGridSpec(
            num_scalar_prefetch=2,
            grid=(heads, tiles),
            in_specs=[tile_in, tile_in, slab_in, slab_in, rim, rim],
            out_specs=[tile_out, tile_out, mid, rim, rim],
            scratch_shapes=[
                pltpu.VMEM((ext, HD), BF16),
                pltpu.VMEM((ext, HD), BF16),
                pltpu.VMEM((ext, HD), F32),
                pltpu.VMEM((ext, HD), F32),
                pltpu.VMEM((SLOTS, TILE, TILE), F32),
            ],
        ),
        out_shape=[
            jax.ShapeDtypeStruct((rows, cols), BF16),
            jax.ShapeDtypeStruct((rows, cols), BF16),
            jax.ShapeDtypeStruct((2, rows, cols), F32),
            jax.ShapeDtypeStruct((2, RIM, cols), BF16),
            jax.ShapeDtypeStruct((2, RIM, cols), F32),
        ],
        compiler_params=pltpu.CompilerParams(
            dimension_semantics=("arbitrary", "arbitrary"), vmem_limit_bytes=40 << 20
        ),
        cost_estimate=pl.CostEstimate(
            flops=pairs * 12 * TILE * TILE * HD,
            bytes_accessed=rows * cols * 40,
            transcendentals=pairs * TILE * TILE,
        ),
    )(place, count, q, g, k, v, far, near)


def swap(x, axis, bit):
    return lax.ppermute(x, axis, [(i, i ^ bit) for i in range(lax.axis_size(axis))])


def shift(x, axis, even_step):
    size = lax.axis_size(axis)
    pairs = [(i, i + (even_step if i % 2 == 0 else -even_step)) for i in range(size)]
    return lax.ppermute(x, axis, [(i, j) for i, j in pairs if 0 <= j < size])


MESH = pl.DeviceIdType.MESH

def mega(
    q_hbm, k_hbm, v_hbm, w_hbm, c_hbm, nb,
    proj_hbm, dq_hbm, dk_hbm, dv_hbm, gw_hbm,
    q, kx, vx, cot, w, g, att, dq, e, scr, st, ak, av,
    far_out, far_in, near_out, near_in, wx_out, wx_in, two_out, two_in, keep, four_out, four_in, gw,
    uz_out, uz_in, u4_out, u4_in, ux_out, ux_in,
    core_out, core_in, y_out, y_in,
    loc_s, out_s, kv_s, kv_r, fw_s, fw_r, cy_s, cy_r, cc_s, cc_r, rf_s, rf_r, rn_s, rn_r,
    wx_s, wx_r, two_s, two_r, four_s, four_r, co_s, co_r, y_s, y_r, u_s, u_r,
    *, seq, norm,
):
    s, h = lax.axis_index("seq"), lax.axis_index("head")
    x, z0, z1 = s % 2, (s // 2) % 2, (s // 4) % 2
    h0, h1 = h % 2, (h // 2) % 2
    beside = (s + 1 - 2 * x, h)
    hop2 = (s + 2 - 4 * z0, h)
    hop4 = (s + 4 - 8 * z1, h)
    mate = (s, h + 1 - 2 * h0)
    across = (s, h + 2 - 4 * h1)
    rows, cols = q.shape
    heads = cols // HD
    tiles = rows // TILE
    width = proj_hbm.shape[1]
    piece = gw_hbm.shape[1]
    scale = 1.0 / math.sqrt(HD)
    c2 = scale * math.log2(math.e)
    up, down = s + 2 - 4 * x, s - 2 + 4 * x
    has_up = (up >= 0) & (up < seq)
    has_down = (down >= 0) & (down < seq)

    def slab(i):
        return pl.ds(pl.multiple_of(i * rows, TILE), rows)

    far_at, near_at, mid_at = slab(2 * x), slab(2 - 2 * x), pl.ds(rows, rows)

    def send(src, dst, sem_s, sem_r, dev):
        return pltpu.make_async_remote_copy(
            src_ref=src, dst_ref=dst, send_sem=sem_s, recv_sem=sem_r,
            device_id=dev, device_id_type=MESH,
        )

    def hcol(i):
        return slice(i * HD, (i + 1) * HD)

    barrier = pltpu.get_barrier_semaphore()
    for dev in (beside, hop4, mate, across):
        pl.semaphore_signal(barrier, inc=1, device_id=dev, device_id_type=MESH)

    @pl.when(s >= 2)
    def _():
        pl.semaphore_signal(barrier, inc=1, device_id=(s - 2, h), device_id_type=MESH)

    @pl.when(s + 2 < seq)
    def _():
        pl.semaphore_signal(barrier, inc=1, device_id=(s + 2, h), device_id_type=MESH)

    local = [pltpu.make_async_copy(c_hbm, cot.at[0], loc_s.at[0]),
             pltpu.make_async_copy(q_hbm, q, loc_s.at[1]),
             pltpu.make_async_copy(w_hbm, w, loc_s.at[2])]
    for i in range(heads):
        local.append(pltpu.make_async_copy(k_hbm.at[:, hcol(i)], kx.at[i, mid_at], loc_s.at[3 + 2 * i]))
        local.append(pltpu.make_async_copy(v_hbm.at[:, hcol(i)], vx.at[i, mid_at], loc_s.at[4 + 2 * i]))
    for copy in local:
        copy.start()

    pl.semaphore_wait(barrier, 4 + (s + seq - 2) // seq + (2 * seq - 3 - s) // seq)

    kv, fw = [], []
    for i in range(heads):
        for n, (src, buf) in enumerate(((k_hbm, kx), (v_hbm, vx))):
            kv.append(send(src.at[:, hcol(i)], buf.at[i, slab(2 * x)], kv_s.at[2 * i + n], kv_r.at[2 * i + n], beside))
            fw.append(send(buf.at[i, near_at], buf.at[i, far_at], fw_s.at[2 * i + n], fw_r.at[2 * i + n], (up, h)))
    tile_rows = [pl.ds(t * TILE, TILE) for t in range(tiles)]
    cy = [send(c_hbm.at[r], cot.at[2, r], cy_s.at[t], cy_r.at[t], across) for t, r in enumerate(tile_rows)]
    cc = [send(cot.at[2, r], cot.at[3, r], cc_s.at[t], cc_r.at[t], mate) for t, r in enumerate(tile_rows)]
    cm = send(c_hbm, cot.at[1], cc_s.at[tiles], cc_r.at[tiles], mate)
    for copy in kv[:2] + cy + [cm] + kv[2:]:
        copy.start()

    @pl.when(jnp.logical_not(has_down))
    def _():
        for i in range(heads):
            kx[i, far_at] = jnp.zeros((rows, HD), BF16)
            vx[i, far_at] = jnp.zeros((rows, HD), BF16)

    def forward_halo(i):
        for n in range(2):
            kv[2 * i + n].wait_recv()

            @pl.when(has_up)
            def _():
                fw[2 * i + n].start()

    def halo(i):
        @pl.when(has_down)
        def _():
            for n in range(2):
                fw[2 * i + n].wait_recv()

    def dead(t, c):
        cand = s * tiles - REACH + t + c
        hit = sum(((nb[t, j] == cand) & (cand >= 0)).astype(jnp.int32) for j in range(SLOTS))
        return (1 - hit).astype(F32) * 1e30

    def tile(t):
        return pl.ds(pl.multiple_of(t * TILE, TILE), TILE)

    def cand(t, c):
        return pl.ds(pl.multiple_of((t + c) * TILE, TILE), TILE)

    spread = 2 * REACH + 1

    def each_tile(step):
        def body(t, carry):
            step(t)
            return carry

        lax.fori_loop(0, tiles, body, 0)

    def fwd(i):
        def step(t):
            at = tile(t)
            qv = q[at, hcol(i)]
            m = jnp.full((8, TILE), -3e38, F32)
            off = [dead(t, c) for c in range(spread)]
            for c in range(spread):
                sc = dot_nt(kx[i, cand(t, c), :], qv)
                scr[0, c] = sc
                m = jnp.maximum(m, jnp.max(sc.reshape(TILE // 8, 8, TILE), axis=0) - off[c])
            m = jnp.max(m, axis=0, keepdims=True) * c2
            total = jnp.zeros((8, TILE), F32)
            acc = jnp.zeros((TILE, HD), F32)
            for c in range(spread):
                p = jnp.exp2(scr[0, c] * c2 - (m + off[c]))
                total = total + jnp.sum(p.reshape(TILE // 8, 8, TILE), axis=0)
                low = p.astype(BF16)
                e[i % 2, t, c] = low
                acc = acc + dot_tn(low, vx[i, cand(t, c), :])
            inv = jnp.broadcast_to(1.0 / jnp.sum(total, axis=0, keepdims=True), (HD, TILE)).T
            att[at, hcol(i)] = (acc * inv).astype(BF16)
            st[i % 2, t] = inv

        each_tile(step)

    def bwd(i):
        ak[i] = jnp.zeros_like(ak[i])
        av[i] = jnp.zeros_like(av[i])

        def step(t):
            at = tile(t)
            qv = q[at, hcol(i)]
            gv = g[at, hcol(i)].astype(F32) * st[i % 2, t]
            delta = jnp.sum((gv * att[at, hcol(i)].astype(F32)).T, axis=0, keepdims=True)
            gb = gv.astype(BF16)
            acc = jnp.zeros((TILE, HD), F32)
            for c in range(spread):
                here = cand(t, c)
                p = e[i % 2, t, c]
                ds = (p.astype(F32) * (dot_nt(vx[i, here, :], gb) - delta)).astype(BF16)
                av[i, here, :] += dot_nn(p, gb)
                ak[i, here, :] += dot_nn(ds, qv)
                acc = acc + dot_tn(ds, kx[i, here, :])
            dq[at, hcol(i)] = (acc * scale).astype(BF16)

        each_tile(step)

    rf = [[send(far_out.at[i, n], far_in.at[i, n], rf_s.at[i, n], rf_r.at[i, n], (down, h)) for n in range(2)]
          for i in range(heads)]
    rn = [[send(near_out.at[i, n], near_in.at[i, n], rn_s.at[i, n], rn_r.at[i, n], beside) for n in range(2)]
          for i in range(heads)]
    part = (lambda i, at: ak[i, at] * scale, lambda i, at: av[i, at])

    def send_far(i):
        @pl.when(has_down)
        def _():
            for n in range(2):
                far_out[i, n] = part[n](i, far_at).astype(BF16)
                rf[i][n].start()

    def relay(i):
        for n in range(2):
            @pl.when(has_up)
            def _():
                rf[i][n].wait_recv()
                near_out[i, n] = (part[n](i, near_at) + far_in[i, n].astype(F32)).astype(BF16)

            @pl.when(jnp.logical_not(has_up))
            def _():
                near_out[i, n] = part[n](i, near_at).astype(BF16)

            rn[i][n].start()

    outs = []

    def write(src, dst):
        copy = pltpu.make_async_copy(src, dst, out_s.at[len(outs)])
        copy.start()
        outs.append(copy)

    def settle(i):
        @pl.when(has_down)
        def _():
            for n in range(2):
                rf[i][n].wait_send()

        for n, dst in enumerate((dk_hbm, dv_hbm)):
            rn[i][n].wait_recv()
            far_out[i, n] = (part[n](i, mid_at) + near_in[i, n].astype(F32)).astype(BF16)
            write(far_out.at[i, n], dst.at[:, hcol(i)])

    def shard(k):
        return (h0 + z0 + k % 2) % 2 + 2 * ((h1 + z1 + k // 2) % 2)

    def term(i, k, side):
        at = pl.ds(pl.multiple_of(side * piece, piece), piece)
        return dot_tn(att[:, hcol(i)], cot[shard(k), :, at])

    rest = heads - 1
    wx = [send(wx_out.at[p], wx_in.at[p], wx_s.at[p], wx_r.at[p], beside) for p in range(rest)]
    twos = [send(two_out.at[p], two_in.at[p], two_s.at[p], two_r.at[p], hop2) for p in range(rest)]
    fours = [send(four_out.at[p], four_in.at[p], four_s.at[p], four_r.at[p], hop4) for p in range(rest)]

    def weight_x(i):
        for k in range(4):
            wx_out[i - 1, k] = term(i, k, 1 - x).astype(BF16)
        wx[i - 1].start()

    def weight_two(i):
        own = [term(i, k, x) for k in range(4)]
        p = i - 1
        wx[p].wait_recv()
        for n, k in enumerate((1, 3)):
            two_out[p, n] = (own[k] + wx_in[p, k].astype(F32)).astype(BF16)
        twos[p].start()
        for n, k in enumerate((0, 2)):
            keep[p, n] = own[k] + wx_in[p, k].astype(F32)

    def weight_four(i):
        p = i - 1
        twos[p].wait_recv()
        four_out[p] = (keep[p, 1] + two_in[p, 1].astype(F32)).astype(BF16)
        fours[p].start()
        keep[p, 0] += two_in[p, 0].astype(F32)

    def weight_done(i):
        p = i - 1
        fours[p].wait_recv()
        gw[hcol(i)] = (keep[p, 0] + four_in[p].astype(F32)) * norm
        write(gw.at[hcol(i)], gw_hbm.at[hcol(i)])

    soon = (h1 + z1) % 2
    uz = [send(uz_out.at[n], uz_in.at[n], u_s.at[j], u_r.at[j], hop2) for j, n in enumerate((soon, 1 - soon))]
    u4 = send(u4_out, u4_in, u_s.at[2], u_r.at[2], hop4)
    ux = send(ux_out, ux_in, u_s.at[3], u_r.at[3], beside)

    def first_two(j):
        n = soon if j == 0 else 1 - soon
        for side in range(2):
            uz_out[n, side] = term(0, 1 + 2 * n, side).astype(BF16)
        uz[j].start()

    def first_four():
        own = [term(0, 2, side) for side in range(2)]
        for j in range(2):
            uz[j].wait_recv()
        for side in range(2):
            u4_out[side] = (own[side] + uz_in[1, side].astype(F32)).astype(BF16)
        u4.start()

    def first_x():
        u4.wait_recv()
        for side, to in ((1 - x, ux_out), (x, gw)):
            total = term(0, 0, side) + uz_in[0, side].astype(F32) + u4_in[side].astype(F32)
            to[:HD] = total.astype(to.dtype)
        ux.start()

    def first_done():
        ux.wait_recv()
        gw[:HD] = (gw[:HD] + ux_in[...].astype(F32)) * norm
        write(gw.at[:HD], gw_hbm.at[:HD])

    def wcols(r):
        b0, b1 = (h0 + r % 2) % 2, (h1 + r // 2) % 2
        return pl.ds(pl.multiple_of((b0 + 2 * b1) * width, width), width)

    def share(t, r):
        return dot_nn(att[tile_rows[t], :], w[:, wcols(r)])

    cores = [[send(core_out.at[n, t], core_in.at[n, t], co_s.at[n, t], co_r.at[n, t], mate) for t in range(tiles)]
             for n in range(2)]
    ys = [send(y_out.at[t], y_in.at[t], y_s.at[t], y_r.at[t], across) for t in range(tiles)]

    def project_out():
        for n, r in enumerate((3, 1)):
            for t in range(tiles):
                core_out[n, t] = share(t, r).astype(BF16)
                cores[n][t].start()
        for t in range(tiles):
            total = share(t, 2)
            cores[0][t].wait_recv()
            y_out[t] = (total + core_in[0, t].astype(F32)).astype(BF16)
            ys[t].start()

    def project_in(t):
        total = share(t, 0)
        cores[1][t].wait_recv()
        ys[t].wait()
        y_out[t] = (total + core_in[1, t].astype(F32) + y_in[t].astype(F32)).astype(BF16)
        write(y_out.at[t], proj_hbm.at[tile_rows[t]])

    def grad_begin(t):
        total = dot_nt(cot[0, tile_rows[t]], w[:, wcols(0)])
        total += dot_nt(cot[1, tile_rows[t]], w[:, wcols(1)])
        for i in range(heads):
            ak[i, tile_rows[t]] = total[:, hcol(i)]

    def grad_end(t):
        total = dot_nt(cot[2, tile_rows[t]], w[:, wcols(2)])
        total += dot_nt(cot[3, tile_rows[t]], w[:, wcols(3)])
        for i in range(heads):
            g[tile_rows[t], hcol(i)] = (ak[i, tile_rows[t]] + total[:, hcol(i)]).astype(BF16)

    forward_halo(0)
    for copy in local:
        copy.wait()
    forward_halo(1)
    halo(0)
    fwd(0)
    cy[0].wait_recv()
    cc[0].start()
    cm.wait_recv()
    first_two(0)
    for t in range(tiles):
        grad_begin(t)
    halo(1)
    forward_halo(2)
    cy[1].wait_recv()
    cc[1].start()
    fwd(1)
    cc[0].wait_recv()
    cc[1].wait_recv()
    for t in range(tiles):
        grad_end(t)
    first_two(1)
    weight_x(1)
    bwd(1)
    send_far(1)
    halo(2)
    forward_halo(3)
    bwd(0)
    fwd(2)
    weight_x(2)
    send_far(0)
    halo(3)
    relay(1)
    weight_two(1)
    first_four()
    fwd(3)
    weight_x(3)
    relay(0)
    weight_two(2)
    bwd(3)
    send_far(3)
    project_out()
    bwd(2)
    write(dq, dq_hbm)
    first_x()
    weight_four(1)
    weight_four(2)
    relay(3)
    send_far(2)
    weight_two(3)
    settle(0)
    relay(2)
    weight_four(3)
    settle(3)
    settle(1)
    for t in range(tiles):
        project_in(t)
    first_done()
    weight_done(2)
    weight_done(1)
    settle(2)
    weight_done(3)

    for copy in outs:
        copy.wait()

    @pl.when(has_up)
    def _():
        for copy in fw:
            copy.wait_send()

    for copy in kv + cy + cc + [cm] + sum(rn, []) + wx + twos + fours + cores[0] + cores[1] + uz + [u4, ux]:
        copy.wait_send()


def mega_call(q, k, v, w, c, nb, seq, norm):
    rows, cols = q.shape
    heads = cols // HD
    tiles = rows // TILE
    width = c.shape[1]
    piece = width * 4 // seq
    rest = heads - 1
    ext = 3 * rows
    spread = 2 * REACH + 1
    hbm = pl.BlockSpec(memory_space=pl.ANY)
    sem = pltpu.SemaphoreType.DMA
    vm = pltpu.VMEM
    return pl.pallas_call(
        functools.partial(mega, seq=seq, norm=norm),
        in_specs=[hbm] * 5 + [pl.BlockSpec(memory_space=pltpu.SMEM)],
        out_specs=[hbm] * 5,
        out_shape=[
            jax.ShapeDtypeStruct((rows, width), BF16),
            jax.ShapeDtypeStruct((rows, cols), BF16),
            jax.ShapeDtypeStruct((rows, cols), BF16),
            jax.ShapeDtypeStruct((rows, cols), BF16),
            jax.ShapeDtypeStruct((cols, piece), F32),
        ],
        scratch_shapes=[
            vm((rows, cols), BF16),
            vm((heads, ext, HD), BF16),
            vm((heads, ext, HD), BF16),
            vm((4, rows, width), BF16),
            vm(w.shape, BF16),
            vm((rows, cols), BF16),
            vm((rows, cols), BF16),
            vm((rows, cols), BF16),
            vm((2, tiles, spread, TILE, TILE), BF16),
            vm((1, spread, TILE, TILE), F32),
            vm((2, tiles, TILE, HD), F32),
            vm((heads, ext, HD), F32),
            vm((heads, ext, HD), F32),
            vm((heads, 2, rows, HD), BF16),
            vm((heads, 2, rows, HD), BF16),
            vm((heads, 2, rows, HD), BF16),
            vm((heads, 2, rows, HD), BF16),
            vm((rest, 4, HD, piece), BF16),
            vm((rest, 4, HD, piece), BF16),
            vm((rest, 2, HD, piece), BF16),
            vm((rest, 2, HD, piece), BF16),
            vm((rest, 2, HD, piece), F32),
            vm((rest, HD, piece), BF16),
            vm((rest, HD, piece), BF16),
            vm((cols, piece), F32),
            vm((2, 2, HD, piece), BF16),
            vm((2, 2, HD, piece), BF16),
            vm((2, HD, piece), BF16),
            vm((2, HD, piece), BF16),
            vm((HD, piece), BF16),
            vm((HD, piece), BF16),
            vm((2, tiles, TILE, width), BF16),
            vm((2, tiles, TILE, width), BF16),
            vm((tiles, TILE, width), BF16),
            vm((tiles, TILE, width), BF16),
            sem((3 + 2 * heads,)), sem((1 + 3 * heads + tiles,)),
            sem((2 * heads,)), sem((2 * heads,)), sem((2 * heads,)), sem((2 * heads,)),
            sem((tiles,)), sem((tiles,)), sem((tiles + 1,)), sem((tiles + 1,)),
            sem((heads, 2)), sem((heads, 2)), sem((heads, 2)), sem((heads, 2)),
            sem((rest,)), sem((rest,)), sem((rest,)), sem((rest,)), sem((rest,)), sem((rest,)),
            sem((2, tiles)), sem((2, tiles)), sem((tiles,)), sem((tiles,)), sem((4,)), sem((4,)),
        ],
        compiler_params=pltpu.CompilerParams(
            collective_id=0, has_side_effects=True, vmem_limit_bytes=62 << 20
        ),
        cost_estimate=pl.CostEstimate(
            flops=16 * rows * cols * width * 3, bytes_accessed=40 << 20, transcendentals=0
        ),
    )(q, k, v, w, c, nb)


def store(n, *refs):
    srcs, dsts, bufs = refs[:n], refs[n : 2 * n], refs[2 * n : 3 * n]
    in_sem, out_sem = refs[3 * n :]
    pairs = []
    for i in range(n):
        step = srcs[i].shape[0] // PARTS
        for j in range(PARTS):
            at = pl.ds(j * step, step)
            pairs.append((
                pltpu.make_async_copy(srcs[i].at[at], bufs[i].at[at], in_sem.at[i, j]),
                pltpu.make_async_copy(bufs[i].at[at], dsts[i].at[at], out_sem.at[i, j]),
            ))
    for load, _ in pairs:
        load.start()
    for load, save in pairs:
        load.wait()
        save.start()
    for _, save in pairs:
        save.wait()


def store_call(arrays):
    hbm = pl.BlockSpec(memory_space=pl.ANY)
    n = len(arrays)
    sems = pltpu.SemaphoreType.DMA((n, PARTS))
    return pl.pallas_call(
        functools.partial(store, n),
        in_specs=[hbm] * n,
        out_specs=[hbm] * n,
        out_shape=[jax.ShapeDtypeStruct(a.shape, a.dtype) for a in arrays],
        scratch_shapes=[pltpu.VMEM(a.shape, a.dtype) for a in arrays] + [sems, sems],
        compiler_params=pltpu.CompilerParams(vmem_limit_bytes=60 << 20),
        cost_estimate=pl.CostEstimate(flops=0, bytes_accessed=8 << 20, transcendentals=0),
    )(*arrays)


def local(queries, key_rows, value_rows, out_weight, cotangent, neighbours):
    rows, columns = queries.shape
    heads = columns // HD
    tiles = rows // TILE
    seq, head = lax.axis_size("seq"), lax.axis_size("head")
    s = lax.axis_index("seq")
    norm = 1.0 / math.sqrt(rows * seq)
    chunks = 2
    per = heads // chunks
    if head == 4 and seq == 8 and heads == 4 and tiles == REACH:
        return store_call(
            mega_call(queries, key_rows, value_rows, out_weight, cotangent, neighbours, seq, norm)
        )

    halos = []
    for n in range(chunks):
        cut = slice(n * per * HD, (n + 1) * per * HD)
        kv = jnp.stack([key_rows[:, cut], value_rows[:, cut]])
        near = swap(kv, "seq", 1)
        far = shift(near, "seq", 2)
        halos.append((far, near))

    full = lax.all_gather(cotangent, "head", axis=1, tiled=True)
    grad_attention = dot_nt(full, out_weight).astype(BF16)

    first = s * tiles - REACH
    alive = neighbours >= 0
    index = jnp.where(alive, neighbours - first, 0)
    span = tiles + REACH
    odd = s % 2 == 1
    turned = jnp.where(index < REACH, index + span, jnp.where(index >= span, index - span, index))
    place = jnp.where(odd, turned, index).reshape(-1).astype(jnp.int32)
    count = jnp.sum(alive, axis=1).astype(jnp.int32)

    atts, dqs, mids, fars, nears = [], [], [], [], []
    for n in range(chunks):
        far, near = halos[n]
        att, dq, mid, rim_far, rim_near = attention_call(
            place, count, queries, grad_attention, key_rows, value_rows, far, near, n * per, per
        )
        atts.append(att)
        dqs.append(dq)
        mids.append(mid)
        fars.append(rim_far)
        nears.append(rim_near)

    grad_queries = jnp.concatenate(dqs, axis=1)
    dks, dvs = [], []
    for n in range(chunks):
        relayed = shift(fars[n], "seq", -2)
        back = swap((nears[n] + relayed.astype(F32)).astype(BF16), "seq", 1)
        done = (mids[n] + back.astype(F32)).astype(BF16)
        dks.append(done[0])
        dvs.append(done[1])
    attention = jnp.concatenate(atts, axis=1)
    projected = lax.psum_scatter(
        dot_nn(attention, out_weight).astype(BF16), "head", scatter_dimension=1, tiled=True
    )
    grad_weight = (
        lax.psum_scatter(
            dot_tn(attention, full).astype(BF16), "seq", scatter_dimension=1, tiled=True
        ).astype(F32)
        * norm
    )
    return (
        projected,
        grad_queries,
        jnp.concatenate(dks, axis=1),
        jnp.concatenate(dvs, axis=1),
        grad_weight,
    )


def solution(mesh):
    both = P("seq", "head")
    return jax.shard_map(
        local,
        mesh=mesh,
        in_specs=(both, both, both, P("head", None), both, P("seq", None)),
        out_specs=(both, both, both, both, P("head", "seq")),
        check_vma=False,
    )
```
